256 devices in a mesh: seq: 32 (over x, y, core), head: 8 (over z).
Axes of the slice: x: 4, y: 4, z: 8, core: 2. Of those that a mesh axis runs over, the one named last changes fastest.
Arguments:
- queries: bfloat16 [32, 8192, 128], P('head', 'seq'), may hold values from -0.5390625 to 0.5390625
- keys: bfloat16 [32, 8192, 128], P('head', 'seq'), may hold values from -0.5390625 to 0.5390625
- values: bfloat16 [32, 8192, 128], P('head', 'seq'), may hold values from -15 to 15
- log_decay: float32 [32, 8192], P('head', 'seq'), may hold values from -1 to 0, as said below
- level_weight: float32 [32, 21, 8192], P('head', None, 'seq'), may hold values from 0.2 to 2
- gate_input: bfloat16 [32, 8192, 128], P('head', 'seq'), may hold values from -6 to 6
- norm_gain: float32 [32, 128], P('head'), may hold values from 0.5 to 1.5
- out_grad: bfloat16 [32, 8192, 128], P('head', 'seq'), may hold values from -15 to 15
Outputs:
- layer_out: bfloat16 [32, 8192, 128], P('head', 'seq')
- grad_queries: bfloat16 [32, 8192, 128], P('head', 'seq')
- grad_keys: bfloat16 [32, 8192, 128], P('head', 'seq')
- grad_values: bfloat16 [32, 8192, 128], P('head', 'seq')
- grad_levels: float32 [32, 21, 8192], P('head', None, 'seq')
- grad_gate: bfloat16 [32, 8192, 128], P('head', 'seq')
- grad_gain: float32 [32, 128], P('head')
The draws below stay inside these ranges and needn't reach their ends.
Inputs may be any that keep to these rules, and one draw needn't show every extreme that they name: `log_decay`: negative logarithms of decays.
All inputs are finite; a program needn't handle non-finite values.
Results may differ from the reference program's by a relative error of at most 0.0051.
Values sent between devices are 32-bit elements; how exact they have to be, the bound alone decides.
No kernel may reach another device: no remote copies, remote signals or barrier semaphores. Data moves between devices by JAX's collectives and lax.ppermute only.
A program may use at most 64 MiB of HBM per device.

```python
import math
import jax
import jax.numpy as jnp
from jax import lax

HEADS = 32
STATE = 128
HEAD_DIM = 128
LEVELS = 21
C_DEV = 256
TOKENS = 8192
N_SEQ = 32


def draw_log_decay(key, part):
    keys = jax.random.split(jax.random.fold_in(key, 11), 7)
    blocks = TOKENS // C_DEV
    share = 0.5
    quick = jax.random.uniform(keys[0], (HEADS, 1)) < share
    quick_rate = jnp.exp(jax.random.uniform(keys[1], (HEADS, 1), minval=jnp.log(1.0 / 50.0), maxval=jnp.log(1.0 / 30.0)))
    slow_rate = jax.random.uniform(keys[2], (HEADS, 1), minval=0.2, maxval=0.8) / TOKENS
    decay_speed = jnp.where(quick, quick_rate, slow_rate)
    multiplier_term = jnp.exp(jax.random.uniform(keys[3], (HEADS, blocks), minval=-0.7, maxval=0.7))
    multiplier_term = jnp.repeat(multiplier_term, C_DEV, axis=1)
    coarse_estimate = jax.random.uniform(keys[4], (HEADS, TOKENS), minval=0.5, maxval=1.5)
    spots = jax.random.randint(keys[5], (3,), 0, TOKENS)
    gate_intensity = jnp.log(jax.random.uniform(keys[6], (3,), minval=0.5, maxval=0.8))
    positioned_rows = jnp.arange(TOKENS)[None, :] == spots[:, None]
    spike_level = jnp.sum(jnp.where(positioned_rows, gate_intensity[:, None], 0.0), axis=0)
    value_entry = -decay_speed * multiplier_term * coarse_estimate + spike_level[None, :]
    return jnp.clip(value_entry, -1.0, -1e-07).astype(jnp.float32)


def draw_values(key, part):
    keys = jax.random.split(jax.random.fold_in(key, 23), 1)
    rising = 1.0 + 2.0 * jnp.arange(HEADS, dtype=jnp.float32)[:, None, None] / max(HEADS - 1, 1)
    base = jnp.clip(jax.random.normal(keys[0], (HEADS, TOKENS, HEAD_DIM)), -5.0, 5.0)
    return (base * rising).astype(jnp.bfloat16)


def draw_out_grad(key, part):
    keys = jax.random.split(jax.random.fold_in(key, 37), 1)
    rising = 1.0 + 2.0 * jnp.arange(TOKENS, dtype=jnp.float32)[None, :, None] / TOKENS
    base = jnp.clip(jax.random.normal(keys[0], (HEADS, TOKENS, HEAD_DIM)), -5.0, 5.0)
    return (base * rising).astype(jnp.bfloat16)


def shard_levels(rng, extent, shards, low, high):
    loudness = 1.0
    for dim, blocks in shards:
        draws = jax.random.uniform(jax.random.fold_in(jax.random.fold_in(rng, 6), dim), (blocks,), jnp.float32, low / len(shards), high / len(shards))
        loudness = loudness * jnp.repeat(jnp.exp(draws), extent[dim] // blocks).reshape((-1,) + (1,) * (len(extent) - 1 - dim))
    return loudness


def bell_draw(own_key, dims, scale, most, shards=(), kind=jnp.bfloat16):
    level = shard_levels(own_key, dims, shards, -0.22, 0.18) if shards else 1.0
    drawn = jax.random.normal(own_key, dims, jnp.float32) * scale * level
    return jnp.minimum(jnp.maximum(drawn, -most), most).astype(kind)


def setup_inputs(seed: int = 0) -> dict:
    seeds = jax.random.split(jax.random.key(seed), 9)
    return {
        "queries": bell_draw(seeds[0], (HEADS, TOKENS, STATE), 0.09, 0.5390625, ((0, 8), (1, 32))),
        "keys": bell_draw(seeds[1], (HEADS, TOKENS, STATE), 0.09, 0.5390625, ((0, 8), (1, 32))),
        "values": draw_values(jax.random.fold_in(seeds[8], 71), 0),
        "log_decay": draw_log_decay(jax.random.fold_in(seeds[8], 71), 0),
        "level_weight": jnp.clip(jnp.exp(math.log(2.0) - 2.3025851 * jax.random.uniform(seeds[4], (HEADS, LEVELS, TOKENS), jnp.float32) ** shard_levels(seeds[4], (HEADS, LEVELS, TOKENS), ((0, 8), (2, 32)), -0.2, 0.2)), 0.2, 2.0),
        "gate_input": bell_draw(seeds[5], (HEADS, TOKENS, HEAD_DIM), 1.0, 6.0, ((0, 8), (1, 32))),
        "norm_gain": jnp.clip(1.0 + 0.1 * jax.random.normal(seeds[6], (HEADS, HEAD_DIM), jnp.float32), 0.5, 1.5),
        "out_grad": draw_out_grad(jax.random.fold_in(seeds[8], 71), 0),
    }


EPSILON = 1e-05
HIGH = lax.Precision.HIGHEST

def level_table(row_start, rows, width, depth):
    row_ids = row_start + lax.iota(jnp.int32, rows)
    column_ids = lax.iota(jnp.int32, width)
    crossed = jnp.bitwise_xor(row_ids[:, None], column_ids[None, :])
    level = jnp.zeros((rows, width), jnp.int32)
    for shift in range(depth):
        level = level + (jnp.right_shift(crossed, shift) > 0).astype(jnp.int32)
    causal = column_ids[None, :] <= row_ids[:, None]
    return (level, causal)

def pair_weights(running, mix_rows, row_start, rows, depth):
    level, causal = level_table(row_start, rows, running.shape[1], depth)
    run_rows = lax.dynamic_slice_in_dim(running, row_start, rows, 1)
    spread = jnp.where(causal[None], run_rows[:, :, None] - running[:, None, :], 0.0)
    decay = jnp.where(causal[None], jnp.exp(spread), 0.0)
    chosen = jnp.zeros_like(decay)
    for place in range(depth + 1):
        chosen = chosen + jnp.where((level == place)[None], mix_rows[:, place, :, None], 0.0)
    return (decay, chosen, level)

def intra_forward(queries, keys, values, running, mix, depth):
    heads, width, state = queries.shape
    rows = min(width, 512)

    def one_block(index):
        start = index * rows
        q_rows = lax.dynamic_slice_in_dim(queries, start, rows, 1)
        mix_rows = lax.dynamic_slice_in_dim(mix, start, rows, 2)
        decay, chosen, level = pair_weights(running, mix_rows, start, rows, depth)
        scores = jnp.einsum('hik,hjk->hij', q_rows.astype(jnp.float32), keys.astype(jnp.float32))
        mixing = (scores * decay * chosen).astype(jnp.bfloat16)
        return jnp.einsum('hij,hjp->hip', mixing.astype(jnp.float32), values.astype(jnp.float32))
    blocks = lax.map(one_block, jnp.arange(width // rows, dtype=jnp.int32))
    return jnp.moveaxis(blocks, 0, 1).reshape(heads, width, -1)

def intra_backward(queries, keys, values, running, mix, grad_mixed, depth):
    heads, width, state = queries.shape
    rows = min(width, 512)
    grad_wide = grad_mixed.astype(jnp.float32)
    keys_wide = keys.astype(jnp.float32)
    values_wide = values.astype(jnp.float32)

    def one_block(carry, index):
        grad_keys, grad_values = carry
        start = index * rows
        q_rows = lax.dynamic_slice_in_dim(queries, start, rows, 1).astype(jnp.float32)
        g_rows = lax.dynamic_slice_in_dim(grad_wide, start, rows, 1)
        mix_rows = lax.dynamic_slice_in_dim(mix, start, rows, 2)
        decay, chosen, level = pair_weights(running, mix_rows, start, rows, depth)
        scores = jnp.einsum('hik,hjk->hij', q_rows, keys_wide)
        weight = decay * chosen
        mixing = (scores * weight).astype(jnp.bfloat16).astype(jnp.float32)
        grad_mixing = jnp.einsum('hip,hjp->hij', g_rows, values_wide)
        grad_scores = (grad_mixing * weight).astype(jnp.bfloat16).astype(jnp.float32)
        grad_q_rows = jnp.einsum('hij,hjk->hik', grad_scores, keys_wide)
        grad_keys = grad_keys + jnp.einsum('hij,hik->hjk', grad_scores, q_rows)
        grad_values = grad_values + jnp.einsum('hij,hip->hjp', mixing, g_rows)
        moved = grad_mixing * scores * decay
        per_level = jnp.stack([lax.optimization_barrier(jnp.sum(jnp.where((level == place)[None], moved, 0.0), axis=2)) for place in range(depth + 1)], axis=1)
        return ((grad_keys, grad_values), (grad_q_rows, per_level))
    start_carry = (jnp.zeros((heads, width, state), jnp.float32), jnp.zeros((heads, width, values.shape[2]), jnp.float32))
    (grad_keys, grad_values), (q_blocks, level_blocks) = lax.scan(one_block, start_carry, jnp.arange(width // rows, dtype=jnp.int32))
    grad_queries = jnp.moveaxis(q_blocks, 0, 1).reshape(heads, width, state)
    grad_levels = jnp.moveaxis(level_blocks, 0, 2).reshape(heads, depth + 1, width)
    return (grad_queries, grad_keys, grad_values, grad_levels)

def route_weights(late, early, before, through, levels):
    spread = before[:, None, :] - through[None, :, :]
    result = []
    for place in range(levels):
        span = 2 ** place
        inside = (late[:, None] // span % 2 == 1) & (early[None, :] // span % 2 == 0) & (late[:, None] // (2 * span) == early[None, :] // (2 * span))
        inside = inside[:, :, None]
        result.append(jnp.where(inside, jnp.exp(jnp.where(inside, spread, 0.0)), 0.0))
    return jnp.stack(result, axis=0)

def reference(queries, keys, values, log_decay, level_weight, gate_input, norm_gain, out_grad):
    heads = queries.shape[0]
    count = N_SEQ
    width = C_DEV
    depth = width.bit_length() - 1
    levels_dev = count.bit_length() - 1

    def stretched(array):
        return jnp.moveaxis(array.reshape((heads, count, width) + array.shape[2:]), 1, 0)

    def joined(array):
        return jnp.moveaxis(array, 0, 1).reshape((heads, count * width) + array.shape[3:])
    q_parts = stretched(queries)
    k_parts = stretched(keys)
    v_parts = stretched(values)
    running = jnp.cumsum(stretched(log_decay), axis=2)
    mixes = jnp.moveaxis(level_weight.reshape(heads, LEVELS, count, width), 2, 0)
    intra_mix = mixes[:, :, :depth + 1]
    inter_mix = mixes[:, :, depth + 1:depth + 1 + levels_dev]
    inner = lax.map(lambda item: intra_forward(item[0], item[1], item[2], item[3], item[4], depth), (q_parts, k_parts, v_parts, running, intra_mix))
    tail = jnp.exp(running[:, :, -1:] - running)
    states = lax.map(lambda item: jnp.einsum('hjk,hjp->hkp', item[0].astype(jnp.float32) * item[2][:, :, None], item[1].astype(jnp.float32), precision=HIGH), (k_parts, v_parts, tail))
    totals = running[:, :, -1]
    through = jnp.cumsum(totals, axis=0)
    before = through - totals
    stretch_ids = jnp.arange(count, dtype=jnp.int32)

    def gather_buckets(index):
        weights = route_weights(index[None], stretch_ids, lax.dynamic_index_in_dim(before, index, 0), through, levels_dev)[:, 0]
        return jnp.einsum('ljh,jhkp->lhkp', weights, states, precision=HIGH)
    buckets = lax.map(gather_buckets, stretch_ids)
    reach = inter_mix * jnp.exp(running)[:, :, None, :]

    def outer_part(item):
        through_q = jnp.einsum('hik,lhkp->lhip', item[0].astype(jnp.float32), item[1], precision=HIGH)
        return jnp.einsum('hli,lhip->hip', item[2], through_q, precision=HIGH)
    outer = lax.map(outer_part, (q_parts, buckets, reach))
    mixed = inner + outer
    gate = stretched(gate_input).astype(jnp.float32)
    sigmoid_gate = jax.nn.sigmoid(gate)
    gate_act = gate * sigmoid_gate
    gated = mixed * gate_act
    total = HEADS * HEAD_DIM
    inverse = lax.rsqrt(lax.optimization_barrier(jnp.sum(gated * gated, axis=(1, 3))) / total + EPSILON)[:, None, :, None]
    gain = norm_gain[None, :, None, :]
    layer_out = (gain * gated * inverse).astype(jnp.bfloat16)
    grad_y = stretched(out_grad).astype(jnp.float32)
    scaled = grad_y * gain
    cross = lax.optimization_barrier(jnp.sum(gated * scaled, axis=(1, 3)))[:, None, :, None]
    grad_gated = inverse * scaled - gated * (inverse * inverse * inverse * cross / total)
    grad_gain = lax.optimization_barrier(jnp.sum(grad_y * gated * inverse, axis=(0, 2)))
    grad_gate = (grad_gated * mixed * sigmoid_gate * (1.0 + gate * (1.0 - sigmoid_gate))).astype(jnp.bfloat16)
    grad_mixed = (grad_gated * gate_act).astype(jnp.bfloat16)
    gq_in, gk_in, gv_in, glev_in = lax.map(lambda item: intra_backward(item[0], item[1], item[2], item[3], item[4], item[5], depth), (q_parts, k_parts, v_parts, running, intra_mix, grad_mixed))

    def inter_back(item):
        q_wide = item[0].astype(jnp.float32)
        grad_wide = item[1].astype(jnp.float32)
        bucket, reach_here, run_here = (item[2], item[3], item[4])
        through_q = jnp.einsum('hik,lhkp->lhip', q_wide, bucket, precision=HIGH)
        grad_levels_here = jnp.exp(run_here)[:, None, :] * jnp.einsum('lhip,hip->hli', through_q, grad_wide, precision=HIGH)
        scaled_q = reach_here[:, :, :, None] * q_wide[:, None]
        bucket_grads = jnp.einsum('hlik,hip->lhkp', scaled_q, grad_wide, precision=HIGH)
        pulled = jnp.einsum('lhkp,hip->lhik', bucket, grad_wide, precision=HIGH)
        grad_q_here = jnp.einsum('hli,lhik->hik', reach_here, pulled, precision=HIGH)
        return (grad_q_here, grad_levels_here, bucket_grads)
    gq_out, glev_out, bucket_grads = lax.map(inter_back, (q_parts, grad_mixed, buckets, reach, running))

    def gather_grads(index):
        weights = route_weights(stretch_ids, index[None], before, lax.dynamic_index_in_dim(through, index, 0), levels_dev)[:, :, 0]
        return jnp.einsum('lch,clhkp->hkp', weights, bucket_grads, precision=HIGH)
    state_grads = lax.map(gather_grads, stretch_ids)
    gk_out = tail[..., None] * jnp.einsum('chkp,chjp->chjk', state_grads, v_parts.astype(jnp.float32), precision=HIGH)
    gv_out = tail[..., None] * jnp.einsum('chkp,chjk->chjp', state_grads, k_parts.astype(jnp.float32), precision=HIGH)
    rest = LEVELS - depth - 1 - levels_dev
    level_parts = jnp.concatenate([glev_in, glev_out, jnp.zeros((count, heads, rest, width), jnp.float32)], axis=2)
    grad_levels = jnp.moveaxis(level_parts, 0, 2).reshape(heads, LEVELS, count * width)
    return (joined(layer_out), joined((gq_in + gq_out).astype(jnp.bfloat16)), joined((gk_in + gk_out).astype(jnp.bfloat16)), joined((gv_in + gv_out).astype(jnp.bfloat16)), grad_levels, joined(grad_gate), grad_gain)
```

```python
import jax
import jax.numpy as jnp
from jax import lax
from jax.experimental import pallas as pl
from jax.experimental.pallas import tpu as pltpu
from jax.sharding import PartitionSpec as P

HEADS = 32
HEAD_DIM = 128
TOTAL = HEADS * HEAD_DIM
EPSILON = 1e-05
HIGH = lax.Precision.HIGHEST
F32 = jnp.float32
BF16 = jnp.bfloat16

LOCAL = 4
WIDTH = 256
DEPTH = 8
INTER = 5
LEVELS = 21
ROWS = HEAD_DIM + 8


def place():
    me = lax.axis_index("seq")
    return me // 8, lax.rem(me // 2, 4), lax.rem(me, 2)


def ring(function):
    pairs = []
    for x in range(4):
        for y in range(4):
            for core in range(2):
                to = function(x, y, core)
                if to is not None:
                    pairs.append(((x * 4 + y) * 2 + core, (to[0] * 4 + to[1]) * 2 + to[2]))
    return pairs


SWAP = ring(lambda x, y, core: (x, y, 1 - core))
UP = ring(lambda x, y, core: (x, y, 1) if core == 0 else None)
DOWN = ring(lambda x, y, core: (x, y, 0) if core == 1 else None)


def along_y(step):
    return ring(lambda x, y, core: (x, (y + step) % 4, core))


def along_x(step):
    return ring(lambda x, y, core: ((x + step) % 4, y, core))


def send(array, pairs):
    return lax.ppermute(array, "seq", pairs)


def flag(condition):
    return condition.astype(F32)


def dot(a, b, dims, precision=None):
    return lax.dot_general(a, b, (dims, ((), ())), precision=precision, preferred_element_type=F32)


NN = ((1,), (0,))
NT = ((1,), (1,))
TN = ((0,), (0,))


def iotas(shape):
    return lax.broadcasted_iota(jnp.int32, shape, 0), lax.broadcasted_iota(jnp.int32, shape, 1)


def state_kernel(decay_ref, level_ref, k_ref, v_ref, keep_ref, send_ref, cols_ref, run_ref, rows_ref):
    core = place()[2]
    early, late = iotas((WIDTH, WIDTH))
    running = dot(decay_ref[...], (early <= late).astype(F32), NN, HIGH)
    run_ref[...] = running
    grown = jnp.exp(running)
    rows_ref[...] = jnp.zeros_like(rows_ref)
    for level in range(INTER):
        rows_ref[4 * level : 4 * level + 4, :] = level_ref[DEPTH + 1 + level] * grown
    rows_ref[20:24, :] = running
    rows_ref[24:28, :] = jnp.exp(running[:, WIDTH - 1 :] - running)
    cols = jnp.transpose(rows_ref[...])
    cols_ref[...] = cols
    for head in range(LOCAL):
        weighted = (v_ref[head].astype(F32) * cols[:, 24 + head : 25 + head]).astype(BF16)
        state = dot(k_ref[head], weighted, TN)
        total = jnp.broadcast_to(running[head : head + 1, WIDTH - 1 :], (4, HEAD_DIM))
        totals = jnp.broadcast_to(running[:, WIDTH - 1 :], (4, HEAD_DIM))

        def put(ref):
            ref[head % 2, 0:HEAD_DIM, :] = state
            ref[head % 2, HEAD_DIM : HEAD_DIM + 4, :] = total
            ref[head % 2, HEAD_DIM + 4 :, :] = totals

        pl.when(core == head // 2)(lambda: put(keep_ref))
        pl.when(core != head // 2)(lambda: put(send_ref))


def intra_kernel(q_ref, k_ref, v_ref, level_ref, run_ref, cols_ref, inner_ref, mix_ref, weight_ref, scored_ref):
    early, late = iotas((WIDTH, WIDTH))
    crossed = jnp.bitwise_xor(early, late)
    causal = early <= late
    for head in range(LOCAL):
        spread = run_ref[head : head + 1, :] - cols_ref[:, 20 + head : 21 + head]
        decay = jnp.where(causal, jnp.exp(jnp.where(causal, spread, 0.0)), 0.0)
        chosen = jnp.broadcast_to(level_ref[0, head : head + 1, :], (WIDTH, WIDTH))
        for level in range(1, DEPTH + 1):
            chosen = jnp.where(crossed >= 2 ** (level - 1), level_ref[level, head : head + 1, :], chosen)
        scored = dot(k_ref[head], q_ref[head], NT)
        weight = decay * chosen
        mixing = (scored * weight).astype(BF16)
        weight_ref[head] = weight
        scored_ref[head] = scored * decay
        mix_ref[head] = mixing
        inner_ref[head] = dot(mixing, v_ref[head], TN)


def order(position, step):
    return lax.rem(position + 4 - step, 4)


def y_kernel(own_ref, one_ref, two_ref, three_ref, next_ref, bucket_ref, info_ref):
    y = place()[1]
    refs = (own_ref, one_ref, two_ref, three_ref)
    where = [order(y, step) for step in range(4)]
    totals = [ref[:, HEAD_DIM : HEAD_DIM + 1, :] for ref in refs]
    by_y = [sum(flag(where[i] == j) * totals[i] for i in range(4)) for j in range(4)]
    carry = jnp.exp(by_y[1])
    whole = jnp.zeros((2, HEAD_DIM, HEAD_DIM), F32)
    pair = jnp.zeros((2, HEAD_DIM, HEAD_DIM), F32)
    for i in range(4):
        state = refs[i][:, 0:HEAD_DIM, :]
        later = sum(flag(j > where[i]) * by_y[j] for j in range(1, 4))
        whole = whole + jnp.exp(later) * state
        if i:
            part = flag(y >= 2) * (flag(where[i] == 1) + flag(where[i] == 0) * carry)
            pair = pair + part * state
    below = sum(flag(j < y) * by_y[j] for j in range(3))
    next_ref[:, 0:HEAD_DIM, :] = whole
    next_ref[:, HEAD_DIM:, :] = jnp.broadcast_to(by_y[0] + by_y[1] + by_y[2] + by_y[3], (2, 8, HEAD_DIM))
    bucket_ref[0, :, 0:HEAD_DIM, :] = flag(lax.rem(y, 2) == 1) * one_ref[:, 0:HEAD_DIM, :]
    bucket_ref[0, :, HEAD_DIM:, :] = jnp.zeros((2, 8, HEAD_DIM), F32)
    bucket_ref[1, :, 0:HEAD_DIM, :] = pair
    bucket_ref[1, :, HEAD_DIM:, :] = jnp.broadcast_to(flag(y == 3) * by_y[2], (2, 8, HEAD_DIM))
    for j in range(4):
        info_ref[:, j : j + 1, :] = by_y[j]
    info_ref[:, 4:8, :] = jnp.broadcast_to(below, (2, 4, HEAD_DIM))


def x_kernel(own_ref, one_ref, two_ref, three_ref, info_ref, bucket_ref, wide_ref):
    x = place()[0]
    refs = (own_ref, one_ref, two_ref, three_ref)
    where = [order(x, step) for step in range(4)]
    totals = [ref[:, HEAD_DIM : HEAD_DIM + 1, :] for ref in refs]
    by_x = [sum(flag(where[i] == j) * totals[i] for i in range(4)) for j in range(4)]
    carry = jnp.exp(by_x[1])
    pair = jnp.zeros((2, HEAD_DIM, HEAD_DIM), F32)
    for i in range(1, 4):
        part = flag(x >= 2) * (flag(where[i] == 1) + flag(where[i] == 0) * carry)
        pair = pair + part * refs[i][:, 0:HEAD_DIM, :]
    below = info_ref[:, 4:5, :]
    bucket_ref[0, :, 0:HEAD_DIM, :] = flag(lax.rem(x, 2) == 1) * one_ref[:, 0:HEAD_DIM, :]
    bucket_ref[0, :, HEAD_DIM:, :] = jnp.broadcast_to(below, (2, 8, HEAD_DIM))
    bucket_ref[1, :, 0:HEAD_DIM, :] = pair
    bucket_ref[1, :, HEAD_DIM:, :] = jnp.broadcast_to(below + flag(x == 3) * by_x[2], (2, 8, HEAD_DIM))
    for j in range(4):
        wide_ref[:, j : j + 1, :] = by_x[j]
        wide_ref[:, 4 + j : 5 + j, :] = by_x[j]


def mixed_kernel(
    q_ref, inner_ref, gate_ref, grad_ref, gain_ref, cols_ref, near_ref, near_other_ref, far_ref, far_other_ref,
    first_ref, rest_ref, mixed_ref, pay_ref, bucket_ref, shift_ref,
):
    core = place()[2]
    odd = flag(core == 1)
    ones = jnp.ones((8, HEAD_DIM), BF16)
    squares = jnp.zeros((8, WIDTH), F32)
    crosses = jnp.zeros((8, WIDTH), F32)
    for head in range(LOCAL):
        slot, mine = head % 2, core == head // 2
        zeroth = rest_ref[slot, 0:HEAD_DIM, :] if head < 2 else first_ref[slot, 0:HEAD_DIM, :]
        earlier = odd * first_ref[0, HEAD_DIM + 4 + head : HEAD_DIM + 5 + head, :]
        parts = [(odd * zeroth).astype(BF16)]
        shift_ref[head] = jnp.ones((8, HEAD_DIM), F32)
        for level in range(1, INTER):
            own, other = (near_ref, near_other_ref) if level < 3 else (far_ref, far_other_ref)
            at = (level - 1) % 2
            chosen = jnp.where(mine, own[at, slot], other[at, slot])
            shift = jnp.exp(earlier + chosen[HEAD_DIM : HEAD_DIM + 1, :])
            shift_ref[head, level : level + 1, :] = shift
            parts.append((chosen[0:HEAD_DIM, :] * shift).astype(BF16))
        bucket = jnp.concatenate(parts, axis=1)
        bucket_ref[head] = bucket
        through = dot(q_ref[head], bucket, NN)
        mixed = inner_ref[head]
        for level in range(INTER):
            at = 4 * level + head
            mixed = mixed + cols_ref[:, at : at + 1] * through[:, HEAD_DIM * level : HEAD_DIM * (level + 1)]
        mixed_ref[head] = mixed
        gate = gate_ref[head].astype(F32)
        gated = mixed * (gate * jax.nn.sigmoid(gate))
        scaled = grad_ref[head].astype(F32) * gain_ref[head : head + 1, :]
        squares = squares + dot(ones, (gated * gated).astype(BF16), NT)
        crosses = crosses + dot(ones, (gated * scaled).astype(BF16), NT)
    for peer in range(8):
        for half in range(2):
            piece = slice(HEAD_DIM * half, HEAD_DIM * (half + 1))
            pay_ref[peer, half : half + 1, :] = squares[0:1, piece]
            pay_ref[peer, 2 + half : 3 + half, :] = crosses[0:1, piece]


def gate_kernel(
    q_ref, mixed_ref, gate_ref, grad_ref, gain_ref, cols_ref, shift_ref, sums_ref,
    out_ref, grad_gate_ref, g_ref, far_keep_ref, far_send_ref, near_keep_ref, near_send_ref, zeroth_ref,
):
    core = place()[2]
    ones = jnp.ones((8, HEAD_DIM), F32)
    wide = [dot(sums_ref[:, i, :], ones, TN, HIGH) for i in range(4)]
    squares = jnp.concatenate(wide[0:2], axis=0)
    crosses = jnp.concatenate(wide[2:4], axis=0)
    inverse = lax.rsqrt(squares * (1.0 / TOTAL) + EPSILON)
    pull = inverse * inverse * inverse * crosses * (1.0 / TOTAL)
    gains = []
    for ref in (far_keep_ref, far_send_ref, near_keep_ref, near_send_ref):
        ref[:, :, HEAD_DIM:, :] = jnp.zeros((2, 2, 8, HEAD_DIM), F32)
    for head in range(LOCAL):
        gain = gain_ref[head : head + 1, :]
        gate = gate_ref[head].astype(F32)
        sigmoid = jax.nn.sigmoid(gate)
        act = gate * sigmoid
        mixed = mixed_ref[head]
        gated = mixed * act
        normed = gated * inverse
        grad = grad_ref[head].astype(F32)
        out_ref[head] = (gain * normed).astype(BF16)
        gains.append(jnp.sum(grad * normed, axis=0, keepdims=True))
        grad_gated = inverse * (grad * gain) - gated * pull
        grad_gate_ref[head] = (grad_gated * mixed * sigmoid * (1.0 + gate * (1.0 - sigmoid))).astype(BF16)
        g = (grad_gated * act).astype(BF16)
        g_ref[head] = g
        wide_g = g.astype(F32)
        reached = [
            (cols_ref[:, 4 * level + head : 4 * level + head + 1] * wide_g).astype(BF16) for level in range(INTER)
        ]
        pulled = dot(q_ref[head], jnp.concatenate(reached, axis=1), TN)
        zeroth_ref[head] = pulled[:, 0:HEAD_DIM]
        scaled = [
            pulled[:, HEAD_DIM * level : HEAD_DIM * (level + 1)] * shift_ref[head, level : level + 1, :]
            for level in range(1, INTER)
        ]

        def put(near, far):
            for level in range(1, INTER):
                ref = near if level < 3 else far
                ref[(level - 1) % 2, head % 2, 0:HEAD_DIM, :] = scaled[level - 1]

        pl.when(core == head // 2)(lambda: put(near_keep_ref, far_keep_ref))
        pl.when(core != head // 2)(lambda: put(near_send_ref, far_send_ref))
    for head in range(LOCAL):
        for ref in (far_keep_ref, far_send_ref):
            for level in range(2):
                ref[level, 0, HEAD_DIM + head : HEAD_DIM + head + 1, :] = gains[head]


def down_kernel(
    own_ref, one_ref, two_ref, three_ref, near_ref, near_other_ref, info_ref, wide_ref,
    m0_ref, m1_ref, m2_ref, m3_ref,
):
    x, y, _ = place()
    refs = (own_ref, one_ref, two_ref, three_ref)
    carry_x = jnp.exp(wide_ref[:, 1:2, :])
    first = x == 0
    c1 = flag(x <= 2)
    c2 = flag(first) * carry_x + flag(x == 1)
    c3 = flag(first) * carry_x
    body = slice(0, HEAD_DIM)
    state = c1 * one_ref[:, body, :] + c2 * two_ref[:, body, :] + c3 * three_ref[:, body, :]
    tails = [ref[:, HEAD_DIM:, :] for ref in refs]
    where = [lax.rem(x + step, 4) for step in range(4)]
    by_x = [sum(flag(where[i] == j) * tails[i] for i in range(4)) for j in range(4)]
    gains = ((by_x[0] + by_x[1]) + by_x[2]) + by_x[3]
    low = near_ref[0, :, body, :] + near_other_ref[0, :, body, :]
    high = near_ref[1, :, body, :] + near_other_ref[1, :, body, :]
    totals = [info_ref[:, j : j + 1, :] for j in range(4)]
    after = [totals[1] + totals[2] + totals[3], totals[2] + totals[3], totals[3], jnp.zeros_like(totals[3])]
    after = [jnp.exp(part) for part in after]
    carry_y = jnp.exp(totals[1])
    for step, ref in enumerate((m0_ref, m1_ref, m2_ref, m3_ref)):
        to = order(y, step)
        message = sum(flag(to == j) * after[j] for j in range(4)) * state
        if step == 1:
            message = message + flag(lax.rem(y, 2) == 1) * low
        if step:
            message = message + flag(y >= 2) * (flag(to == 1) + flag(to == 0) * carry_y) * high
        ref[:, body, :] = message
        ref[:, HEAD_DIM:, :] = gains


def backward_kernel(
    q_ref, k_ref, v_ref, g_ref, mix_ref, weight_ref, scored_ref, bucket_ref, cols_ref, run_ref,
    grad_q_ref, grad_k_ref, grad_v_ref, levels_ref,
):
    early, late = iotas((WIDTH, WIDTH))
    crossed = jnp.bitwise_xor(early, late)
    ones = jnp.ones((8, HEAD_DIM), BF16)
    for level in range(DEPTH + 1 + INTER, LEVELS):
        levels_ref[level] = jnp.zeros((LOCAL, WIDTH), F32)
    for head in range(LOCAL):
        q, k, v, g = q_ref[head], k_ref[head], v_ref[head], g_ref[head]
        grad_mixing = dot(v, g, NT)
        grad_scores = (grad_mixing * weight_ref[head]).astype(BF16)
        grad_k_ref[head] = dot(grad_scores, q, NN)
        grad_v_ref[head] = dot(mix_ref[head], g, NN)
        grad_q = dot(grad_scores, k, TN)
        moved = grad_mixing * scored_ref[head]
        for level in range(DEPTH + 1):
            inside = crossed == 0
            if level:
                inside = (crossed >= 2 ** (level - 1)) & (crossed < 2**level)
            levels_ref[level, head : head + 1, :] = jnp.sum(jnp.where(inside, moved, 0.0), axis=0, keepdims=True)
        wide_q = q.astype(F32)
        grown = jnp.exp(run_ref[head : head + 1, :])
        for level in range(INTER):
            pulled = dot(g, bucket_ref[head, :, HEAD_DIM * level : HEAD_DIM * (level + 1)], NT)
            at = 4 * level + head
            grad_q = grad_q + cols_ref[:, at : at + 1] * pulled
            sums = dot(ones, (wide_q * pulled).astype(BF16), NT)
            levels_ref[DEPTH + 1 + level, head : head + 1, :] = grown * sums[0:1, :]
        grad_q_ref[head] = grad_q.astype(BF16)


def final_kernel(
    k_ref, v_ref, cols_ref, half_ref, other_ref, zeroth_ref, first_ref, grad_k_ref, grad_v_ref, out_k_ref, out_v_ref
):
    core = place()[2]
    even = core == 0
    for head in range(LOCAL):
        slot = head % 2
        half = jnp.where(core == head // 2, half_ref[slot, 0:HEAD_DIM, :], other_ref[slot, 0:HEAD_DIM, :])
        carry = jnp.exp(first_ref[0, HEAD_DIM + 4 + head : HEAD_DIM + 5 + head, :])
        state = jnp.where(even, carry * half + zeroth_ref[head], half).astype(BF16)
        tail = cols_ref[:, 24 + head : 25 + head]
        out_k_ref[head] = (grad_k_ref[head] + tail * dot(v_ref[head], state, NT)).astype(BF16)
        out_v_ref[head] = (grad_v_ref[head] + tail * dot(k_ref[head], state, NN)).astype(BF16)


def call(kernel, outs, *args, scratch=(), flops=0, name=None):
    size = sum(a.size * a.dtype.itemsize for a in args)
    shapes = [jax.ShapeDtypeStruct(shape, kind) for shape, kind in outs]
    size += sum(s.size * s.dtype.itemsize for s in shapes)
    return pl.pallas_call(
        kernel,
        out_shape=shapes,
        scratch_shapes=list(scratch),
        cost_estimate=pl.CostEstimate(flops=flops, bytes_accessed=size, transcendentals=0),
        compiler_params=pltpu.CompilerParams(vmem_limit_bytes=40 * 2**20),
        name=name,
    )(*args)


def local(queries, keys, values, log_decay, level_weight, gate_input, norm_gain, out_grad):
    x, y, core = place()
    level_rows = jnp.transpose(level_weight, (1, 0, 2))
    message = ((2, ROWS, HEAD_DIM), F32)
    double = ((2, 2, ROWS, HEAD_DIM), F32)
    tokens = (LOCAL, WIDTH, HEAD_DIM)
    square = (LOCAL, WIDTH, WIDTH)
    info = ((2, 8, HEAD_DIM), F32)
    in_body = lax.broadcasted_iota(jnp.int32, (2, ROWS, HEAD_DIM), 1) < HEAD_DIM

    keep, away, cols, running = call(
        state_kernel,
        [message, message, ((WIDTH, HEAD_DIM), F32), ((LOCAL, WIDTH), F32)],
        log_decay, level_rows, keys, values,
        scratch=[pltpu.VMEM((HEAD_DIM, WIDTH), F32)],
        name="state",
    )
    first = send(away, SWAP)
    before = jnp.where(core == 1, first, keep)
    after = jnp.where(core == 1, keep, first)
    chip = jnp.where(in_body, jnp.exp(after[:, HEAD_DIM : HEAD_DIM + 1]) * before + after, before + after)
    from_y = [send(chip, along_y(step)) for step in (1, 2, 3)]
    rest = send(keep, UP)
    inner, mixing, weight, scored = call(
        intra_kernel,
        [(tokens, F32), (square, BF16), (square, F32), (square, F32)],
        queries, keys, values, level_rows, running, cols,
        flops=10**9,
        name="intra",
    )
    row, near, totals_y = call(y_kernel, [message, double, info], chip, *from_y, name="up_y")
    from_x = [send(row, along_x(step)) for step in (1, 2, 3)]
    near_other = send(near, SWAP)
    far, totals_x = call(x_kernel, [double, info], row, *from_x, totals_y, name="up_x")
    far_other = send(far, SWAP)
    mixed, pay, bucket, shift = call(
        mixed_kernel,
        [(tokens, F32), ((8, 4, HEAD_DIM), F32), ((LOCAL, HEAD_DIM, INTER * HEAD_DIM), BF16), ((LOCAL, 8, HEAD_DIM), F32)],
        queries, inner, gate_input, out_grad, norm_gain, cols, near, near_other, far, far_other, first, rest,
        name="mixed",
    )
    sums = lax.all_to_all(pay, "head", 0, 0, tiled=True)
    layer_out, grad_gate, grad_mixed, far_keep, far_away, near_keep, near_away, zeroth = call(
        gate_kernel,
        [(tokens, BF16)] * 3 + [double] * 4 + [((LOCAL, HEAD_DIM, HEAD_DIM), F32)],
        queries, mixed, gate_input, out_grad, norm_gain, cols, shift, sums,
        name="gate",
    )
    far_sum = far_keep + send(far_away, SWAP)
    to_one = jnp.where(lax.rem(x, 2) == 1, far_sum[0], far_sum[1])
    to_far = far_sum[1]
    back_x = [send(to_one, along_x(-1)), send(to_far, along_x(-2)), send(to_far, along_x(-3))]
    near_back = send(near_away, SWAP)
    zeroth_back = send(zeroth, DOWN)
    grad_queries, grad_k, grad_v, levels = call(
        backward_kernel,
        [(tokens, BF16), (tokens, F32), (tokens, F32), ((LEVELS, LOCAL, WIDTH), F32)],
        queries, keys, values, grad_mixed, mixing, weight, scored, bucket, cols, running,
        flops=10**9,
        name="backward",
    )
    messages = call(
        down_kernel, [message] * 4, to_far, *back_x, near_keep, near_back, totals_y, totals_x, name="down"
    )
    back_y = [messages[0]] + [send(messages[step], along_y(-step)) for step in (1, 2, 3)]
    by_y = [
        jnp.where(y == j, back_y[0], jnp.where(lax.rem(y + 1, 4) == j, back_y[1], jnp.where(lax.rem(y + 2, 4) == j, back_y[2], back_y[3])))
        for j in range(4)
    ]
    half = ((by_y[0] + by_y[1]) + by_y[2]) + by_y[3]
    half_other = send(half, SWAP)
    grad_keys, grad_values = call(
        final_kernel,
        [(tokens, BF16)] * 2,
        keys, values, cols, half, half_other, zeroth_back, first, grad_k, grad_v,
        name="final",
    )
    grad_gain = half[0, HEAD_DIM : HEAD_DIM + LOCAL]
    grad_levels = jnp.transpose(levels, (1, 0, 2))
    return (layer_out, grad_queries, grad_keys, grad_values, grad_levels, grad_gate, grad_gain)


def solution(mesh):
    rows = P("head", "seq", None)
    in_specs = (rows, rows, rows, P("head", "seq"), P("head", None, "seq"), rows, P("head", None), rows)
    out_specs = (rows, rows, rows, rows, P("head", None, "seq"), rows, P("head", None))
    return jax.shard_map(local, mesh=mesh, in_specs=in_specs, out_specs=out_specs, check_vma=False)
```

```python
import jax
import jax.numpy as jnp
from jax import lax
from jax.experimental import pallas as pl
from jax.experimental.pallas import tpu as pltpu
from jax.sharding import PartitionSpec as P


HEADS = 32
HEAD_DIM = 128
TOTAL = HEADS * HEAD_DIM
EPSILON = 1e-05
HIGH = lax.Precision.HIGHEST
F32 = jnp.float32
BF16 = jnp.bfloat16

LOCAL = 4
WIDTH = 256
DEPTH = 8
INTER = 5
LEVELS = 21
ROWS = HEAD_DIM + 8


def place():
    me = lax.axis_index("seq")
    return me // 8, lax.rem(me // 2, 4), lax.rem(me, 2)


def ring(function):
    pairs = []
    for x in range(4):
        for y in range(4):
            for core in range(2):
                to = function(x, y, core)
                if to is not None:
                    pairs.append(((x * 4 + y) * 2 + core, (to[0] * 4 + to[1]) * 2 + to[2]))
    return pairs


SWAP = ring(lambda x, y, core: (x, y, 1 - core))
UP = ring(lambda x, y, core: (x, y, 1) if core == 0 else None)
DOWN = ring(lambda x, y, core: (x, y, 0) if core == 1 else None)


def along_y(step):
    return ring(lambda x, y, core: (x, (y + step) % 4, core))


def along_x(step):
    return ring(lambda x, y, core: ((x + step) % 4, y, core))


def send(array, pairs):
    return lax.ppermute(array, "seq", pairs)


def split(array):
    high = array.astype(BF16)
    return high, (array - high.astype(F32)).astype(BF16)


def flag(condition):
    return condition.astype(F32)


def dot(a, b, dims, precision=None):
    return lax.dot_general(a, b, (dims, ((), ())), precision=precision, preferred_element_type=F32)


NN = ((1,), (0,))
NT = ((1,), (1,))
TN = ((0,), (0,))


def iotas(shape):
    return lax.broadcasted_iota(jnp.int32, shape, 0), lax.broadcasted_iota(jnp.int32, shape, 1)


def state_kernel(decay_ref, k_hbm, v_hbm, keep_ref, send_ref, run_ref, k_ref, v_ref, rows_ref, sems):
    copies = [
        pltpu.make_async_copy(source, to, sems.at[i])
        for i, (source, to) in enumerate(((v_hbm, v_ref), (k_hbm, k_ref)))
    ]
    for copy in copies:
        copy.start()
    core = place()[2]
    early, late = iotas((WIDTH, WIDTH))
    upper = (early <= late).astype(F32).astype(BF16)
    decay = decay_ref[...]
    first = decay.astype(BF16).astype(F32)
    second = (decay - first).astype(BF16).astype(F32)
    rows_ref[0:4, :] = first
    rows_ref[4:8, :] = second
    rows_ref[8:12, :] = decay - first - second
    rows_ref[12:16, :] = jnp.zeros((4, WIDTH), F32)
    parts = dot(rows_ref[...].astype(BF16), upper, NN)
    running = parts[0:4, :] + parts[4:8, :] + parts[8:12, :]
    run_ref[...] = running
    rows_ref[0:4, :] = jnp.exp(running[:, WIDTH - 1 :] - running)
    tails = jnp.transpose(rows_ref[...])
    for copy in copies:
        copy.wait()
    for head in range(LOCAL):
        weighted = v_ref[head].astype(F32) * tails[:, head : head + 1]
        both = dot(k_ref[head], jnp.concatenate(split(weighted), axis=1), TN)
        state = both[:, 0:HEAD_DIM] + both[:, HEAD_DIM:]
        total = jnp.broadcast_to(running[head : head + 1, WIDTH - 1 :], (4, HEAD_DIM))
        totals = jnp.broadcast_to(running[:, WIDTH - 1 :], (4, HEAD_DIM))

        def put(ref):
            ref[head % 2, 0:HEAD_DIM, :] = state
            ref[head % 2, HEAD_DIM : HEAD_DIM + 4, :] = total
            ref[head % 2, HEAD_DIM + 4 :, :] = totals

        pl.when(core == head // 2)(lambda: put(keep_ref))
        pl.when(core != head // 2)(lambda: put(send_ref))


def pair_kernel(keep_ref, first_ref, chip_ref):
    late = place()[2] == 1
    before = jnp.where(late, first_ref[...], keep_ref[...])
    after = jnp.where(late, keep_ref[...], first_ref[...])
    carry = jnp.exp(after[:, HEAD_DIM : HEAD_DIM + 1, :])
    chip_ref[:, 0:HEAD_DIM, :] = carry * before[:, 0:HEAD_DIM, :] + after[:, 0:HEAD_DIM, :]
    chip_ref[:, HEAD_DIM:, :] = before[:, HEAD_DIM:, :] + after[:, HEAD_DIM:, :]


def intra_kernel(
    q_ref, k_ref, v_ref, level_ref, run_ref, inner_ref, mix_ref, weight_ref, scored_ref, cols_ref, rows_ref
):
    running = run_ref[...]
    grown = jnp.exp(running)
    rows_ref[...] = jnp.zeros_like(rows_ref)
    for level in range(INTER):
        rows_ref[4 * level : 4 * level + 4, :] = level_ref[DEPTH + 1 + level] * grown
    rows_ref[20:24, :] = running
    rows_ref[24:28, :] = jnp.exp(running[:, WIDTH - 1 :] - running)
    cols_ref[...] = jnp.transpose(rows_ref[...])
    early, late = iotas((WIDTH, WIDTH))
    crossed = jnp.bitwise_xor(early, late)
    causal = early <= late
    for head in range(LOCAL):
        spread = run_ref[head : head + 1, :] - cols_ref[:, 20 + head : 21 + head]
        decay = jnp.where(causal, jnp.exp(jnp.where(causal, spread, 0.0)), 0.0)
        chosen = jnp.broadcast_to(level_ref[0, head : head + 1, :], (WIDTH, WIDTH))
        for level in range(1, DEPTH + 1):
            chosen = jnp.where(crossed >= 2 ** (level - 1), level_ref[level, head : head + 1, :], chosen)
        scored = dot(k_ref[head], q_ref[head], NT)
        weight = decay * chosen
        mixing = (scored * weight).astype(BF16)
        weight_ref[head] = weight
        scored_ref[head] = scored * decay
        mix_ref[head] = mixing
        inner_ref[head] = dot(mixing, v_ref[head], TN)


def order(position, step):
    return lax.rem(position + 4 - step, 4)


def y_kernel(own_ref, one_ref, two_ref, three_ref, next_ref, bucket_ref, info_ref):
    y = place()[1]
    refs = (own_ref, one_ref, two_ref, three_ref)
    where = [order(y, step) for step in range(4)]
    totals = [ref[:, HEAD_DIM : HEAD_DIM + 1, :] for ref in refs]
    by_y = [sum(flag(where[i] == j) * totals[i] for i in range(4)) for j in range(4)]
    carry = jnp.exp(by_y[1])
    whole = jnp.zeros((2, HEAD_DIM, HEAD_DIM), F32)
    pair = jnp.zeros((2, HEAD_DIM, HEAD_DIM), F32)
    for i in range(4):
        state = refs[i][:, 0:HEAD_DIM, :]
        later = sum(flag(j > where[i]) * by_y[j] for j in range(1, 4))
        whole = whole + jnp.exp(later) * state
        if i:
            part = flag(y >= 2) * (flag(where[i] == 1) + flag(where[i] == 0) * carry)
            pair = pair + part * state
    below = sum(flag(j < y) * by_y[j] for j in range(3))
    next_ref[:, 0:HEAD_DIM, :] = whole
    next_ref[:, HEAD_DIM:, :] = jnp.broadcast_to(by_y[0] + by_y[1] + by_y[2] + by_y[3], (2, 8, HEAD_DIM))
    bucket_ref[0, :, 0:HEAD_DIM, :] = flag(lax.rem(y, 2) == 1) * one_ref[:, 0:HEAD_DIM, :]
    bucket_ref[0, :, HEAD_DIM:, :] = jnp.zeros((2, 8, HEAD_DIM), F32)
    bucket_ref[1, :, 0:HEAD_DIM, :] = pair
    bucket_ref[1, :, HEAD_DIM:, :] = jnp.broadcast_to(flag(y == 3) * by_y[2], (2, 8, HEAD_DIM))
    for j in range(4):
        info_ref[:, j : j + 1, :] = by_y[j]
    info_ref[:, 4:8, :] = jnp.broadcast_to(below, (2, 4, HEAD_DIM))


def x_kernel(own_ref, one_ref, two_ref, three_ref, info_ref, bucket_ref, wide_ref):
    x = place()[0]
    refs = (own_ref, one_ref, two_ref, three_ref)
    where = [order(x, step) for step in range(4)]
    totals = [ref[:, HEAD_DIM : HEAD_DIM + 1, :] for ref in refs]
    by_x = [sum(flag(where[i] == j) * totals[i] for i in range(4)) for j in range(4)]
    carry = jnp.exp(by_x[1])
    pair = jnp.zeros((2, HEAD_DIM, HEAD_DIM), F32)
    for i in range(1, 4):
        part = flag(x >= 2) * (flag(where[i] == 1) + flag(where[i] == 0) * carry)
        pair = pair + part * refs[i][:, 0:HEAD_DIM, :]
    below = info_ref[:, 4:5, :]
    bucket_ref[0, :, 0:HEAD_DIM, :] = flag(lax.rem(x, 2) == 1) * one_ref[:, 0:HEAD_DIM, :]
    bucket_ref[0, :, HEAD_DIM:, :] = jnp.broadcast_to(below, (2, 8, HEAD_DIM))
    bucket_ref[1, :, 0:HEAD_DIM, :] = pair
    bucket_ref[1, :, HEAD_DIM:, :] = jnp.broadcast_to(below + flag(x == 3) * by_x[2], (2, 8, HEAD_DIM))
    for j in range(4):
        wide_ref[:, j : j + 1, :] = by_x[j]
        wide_ref[:, 4 + j : 5 + j, :] = by_x[j]


def mixed_kernel(
    q_ref, inner_ref, gate_ref, grad_ref, gain_ref, cols_ref, near_ref, near_other_ref, far_ref, far_other_ref,
    first_ref, rest_ref, mixed_ref, pay_ref, bucket_ref, finer_ref, shift_ref,
):
    core = place()[2]
    odd = flag(core == 1)
    ones = jnp.ones((8, HEAD_DIM), BF16)
    squares = jnp.zeros((8, WIDTH), F32)
    crosses = jnp.zeros((8, WIDTH), F32)
    for head in range(LOCAL):
        slot, mine = head % 2, core == head // 2
        zeroth = rest_ref[slot, 0:HEAD_DIM, :] if head < 2 else first_ref[slot, 0:HEAD_DIM, :]
        earlier = odd * first_ref[0, HEAD_DIM + 4 + head : HEAD_DIM + 5 + head, :]
        parts = [split(odd * zeroth)]
        shift_ref[head] = jnp.ones((8, HEAD_DIM), F32)
        for level in range(1, INTER):
            own, other = (near_ref, near_other_ref) if level < 3 else (far_ref, far_other_ref)
            at = (level - 1) % 2
            chosen = jnp.where(mine, own[at, slot], other[at, slot])
            shift = jnp.exp(earlier + chosen[HEAD_DIM : HEAD_DIM + 1, :])
            shift_ref[head, level : level + 1, :] = shift
            parts.append(split(chosen[0:HEAD_DIM, :] * shift))
        bucket, finer = (jnp.concatenate([part[i] for part in parts], axis=1) for i in range(2))
        bucket_ref[head] = bucket
        finer_ref[head] = finer
        through = dot(q_ref[head], bucket, NN) + dot(q_ref[head], finer, NN)
        mixed = inner_ref[head]
        for level in range(INTER):
            at = 4 * level + head
            mixed = mixed + cols_ref[:, at : at + 1] * through[:, HEAD_DIM * level : HEAD_DIM * (level + 1)]
        mixed_ref[head] = mixed
        gate = gate_ref[head].astype(F32)
        gated = mixed * (gate * jax.nn.sigmoid(gate))
        scaled = grad_ref[head].astype(F32) * gain_ref[head : head + 1, :]
        squares = squares + dot(ones, (gated * gated).astype(BF16), NT)
        crosses = crosses + dot(ones, (gated * scaled).astype(BF16), NT)
    for peer in range(8):
        for half in range(2):
            piece = slice(HEAD_DIM * half, HEAD_DIM * (half + 1))
            pay_ref[peer, half : half + 1, :] = squares[0:1, piece]
            pay_ref[peer, 2 + half : 3 + half, :] = crosses[0:1, piece]


def gate_kernel(
    q_ref, mixed_ref, gate_ref, grad_ref, gain_ref, cols_ref, shift_ref, sums_ref,
    g_ref, scale_ref, keep_ref, send_ref,
):
    x, _, core = place()
    ones = jnp.ones((8, HEAD_DIM), F32)
    wide = [dot(sums_ref[:, i, :], ones, TN, HIGH) for i in range(4)]
    squares = jnp.concatenate(wide[0:2], axis=0)
    crosses = jnp.concatenate(wide[2:4], axis=0)
    inverse = lax.rsqrt(squares * (1.0 / TOTAL) + EPSILON)
    pull = inverse * inverse * inverse * crosses * (1.0 / TOTAL)
    scale_ref[0] = inverse
    scale_ref[1] = pull
    gains = []
    for ref in (keep_ref, send_ref):
        ref[:, :, HEAD_DIM:, :] = jnp.zeros((2, 2, 8, HEAD_DIM), F32)
    for head in range(LOCAL):
        gate = gate_ref[head].astype(F32)
        act = gate * jax.nn.sigmoid(gate)
        gated = mixed_ref[head] * act
        grad = grad_ref[head].astype(F32)
        gains.append(jnp.sum(grad * (gated * inverse), axis=0, keepdims=True))
        grad_gated = inverse * (grad * gain_ref[head : head + 1, :]) - gated * pull
        g = (grad_gated * act).astype(BF16)
        g_ref[head] = g
        far = reached(q_ref[head], g.astype(F32), cols_ref, shift_ref, head, (3, 4))
        near = jnp.where(lax.rem(x, 2) == 1, far[0], far[1])

        def put(ref):
            ref[0, head % 2, 0:HEAD_DIM, :] = near
            ref[1, head % 2, 0:HEAD_DIM, :] = far[1]

        pl.when(core == head // 2)(lambda: put(keep_ref))
        pl.when(core != head // 2)(lambda: put(send_ref))
    for head in range(LOCAL):
        for ref in (keep_ref, send_ref):
            ref[0, 0, HEAD_DIM + head : HEAD_DIM + head + 1, :] = gains[head]
            ref[1, 0, HEAD_DIM + head : HEAD_DIM + head + 1, :] = gains[head]


def reached(q, g, cols_ref, shift_ref, head, levels):
    parts = [split(cols_ref[:, 4 * level + head : 4 * level + head + 1] * g) for level in levels]
    both = dot(q, jnp.concatenate([part for pair in parts for part in pair], axis=1), TN)
    found = []
    for i, level in enumerate(levels):
        at = 2 * HEAD_DIM * i
        grad = both[:, at : at + HEAD_DIM] + both[:, at + HEAD_DIM : at + 2 * HEAD_DIM]
        found.append(grad * shift_ref[head, level : level + 1, :])
    return found


def meet_kernel(keep_ref, other_ref, near_ref, far_ref):
    near_ref[...] = keep_ref[0] + other_ref[0]
    far_ref[...] = keep_ref[1] + other_ref[1]


def close_kernel(
    q_ref, g_ref, mixed_ref, gate_ref, grad_ref, gain_ref, cols_ref, shift_ref, scale_ref,
    out_ref, grad_gate_ref, keep_ref, send_ref, zeroth_ref,
):
    core = place()[2]
    inverse, pull = scale_ref[0], scale_ref[1]
    for ref in (keep_ref, send_ref):
        ref[:, :, HEAD_DIM:, :] = jnp.zeros((2, 2, 8, HEAD_DIM), F32)
    for head in range(LOCAL):
        near = reached(q_ref[head], g_ref[head].astype(F32), cols_ref, shift_ref, head, (0, 1, 2))
        zeroth_ref[head] = near[0]

        def put(ref):
            ref[0, head % 2, 0:HEAD_DIM, :] = near[1]
            ref[1, head % 2, 0:HEAD_DIM, :] = near[2]

        pl.when(core == head // 2)(lambda: put(keep_ref))
        pl.when(core != head // 2)(lambda: put(send_ref))
    for head in range(LOCAL):
        gain = gain_ref[head : head + 1, :]
        gate = gate_ref[head].astype(F32)
        sigmoid = jax.nn.sigmoid(gate)
        mixed = mixed_ref[head]
        gated = mixed * (gate * sigmoid)
        out_ref[head] = (gain * (gated * inverse)).astype(BF16)
        grad_gated = inverse * (grad_ref[head].astype(F32) * gain) - gated * pull
        grad_gate_ref[head] = (grad_gated * mixed * sigmoid * (1.0 + gate * (1.0 - sigmoid))).astype(BF16)


def down_kernel(
    own_ref, one_ref, two_ref, three_ref, near_ref, near_other_ref, info_ref, wide_ref,
    m0_ref, m1_ref, m2_ref, m3_ref,
):
    x, y, _ = place()
    refs = (own_ref, one_ref, two_ref, three_ref)
    carry_x = jnp.exp(wide_ref[:, 1:2, :])
    first = x == 0
    c1 = flag(x <= 2)
    c2 = flag(first) * carry_x + flag(x == 1)
    c3 = flag(first) * carry_x
    body = slice(0, HEAD_DIM)
    state = c1 * one_ref[:, body, :] + c2 * two_ref[:, body, :] + c3 * three_ref[:, body, :]
    tails = [ref[:, HEAD_DIM:, :] for ref in refs]
    where = [lax.rem(x + step, 4) for step in range(4)]
    by_x = [sum(flag(where[i] == j) * tails[i] for i in range(4)) for j in range(4)]
    gains = ((by_x[0] + by_x[1]) + by_x[2]) + by_x[3]
    low = near_ref[0, :, body, :] + near_other_ref[0, :, body, :]
    high = near_ref[1, :, body, :] + near_other_ref[1, :, body, :]
    totals = [info_ref[:, j : j + 1, :] for j in range(4)]
    after = [totals[1] + totals[2] + totals[3], totals[2] + totals[3], totals[3], jnp.zeros_like(totals[3])]
    after = [jnp.exp(part) for part in after]
    carry_y = jnp.exp(totals[1])
    for step, ref in enumerate((m0_ref, m1_ref, m2_ref, m3_ref)):
        to = order(y, step)
        message = sum(flag(to == j) * after[j] for j in range(4)) * state
        if step == 1:
            message = message + flag(lax.rem(y, 2) == 1) * low
        if step:
            message = message + flag(y >= 2) * (flag(to == 1) + flag(to == 0) * carry_y) * high
        ref[:, body, :] = message
        ref[:, HEAD_DIM:, :] = gains


def backward_kernel(
    q_ref, k_ref, v_ref, g_ref, mix_ref, weight_ref, scored_ref, bucket_ref, finer_ref, cols_ref, run_ref,
    grad_q_ref, grad_k_ref, grad_v_ref, levels_ref,
):
    early, late = iotas((WIDTH, WIDTH))
    crossed = jnp.bitwise_xor(early, late)
    ones = jnp.ones((8, HEAD_DIM), BF16)
    for level in range(DEPTH + 1 + INTER, LEVELS):
        levels_ref[level] = jnp.zeros((LOCAL, WIDTH), F32)
    for head in range(LOCAL):
        q, k, v, g = q_ref[head], k_ref[head], v_ref[head], g_ref[head]
        grad_mixing = dot(v, g, NT)
        grad_scores = (grad_mixing * weight_ref[head]).astype(BF16)
        grad_k_ref[head] = dot(grad_scores, q, NN)
        grad_v_ref[head] = dot(mix_ref[head], g, NN)
        grad_q = dot(grad_scores, k, TN)
        moved = grad_mixing * scored_ref[head]
        for level in range(DEPTH + 1):
            inside = crossed == 0
            if level:
                inside = (crossed >= 2 ** (level - 1)) & (crossed < 2**level)
            levels_ref[level, head : head + 1, :] = jnp.sum(jnp.where(inside, moved, 0.0), axis=0, keepdims=True)
        wide_q = q.astype(F32)
        grown = jnp.exp(run_ref[head : head + 1, :])
        for level in range(INTER):
            piece = slice(HEAD_DIM * level, HEAD_DIM * (level + 1))
            pulled = dot(g, bucket_ref[head, :, piece], NT) + dot(g, finer_ref[head, :, piece], NT)
            at = 4 * level + head
            grad_q = grad_q + cols_ref[:, at : at + 1] * pulled
            high, low = split(wide_q * pulled)
            sums = dot(ones, high, NT) + dot(ones, low, NT)
            levels_ref[DEPTH + 1 + level, head : head + 1, :] = grown * sums[0:1, :]
        grad_q_ref[head] = grad_q.astype(BF16)


def join_kernel(own_ref, one_ref, two_ref, three_ref, half_ref, gain_ref):
    y = place()[1]
    refs = (own_ref, one_ref, two_ref, three_ref)
    where = [lax.rem(y + step, 4) for step in range(4)]
    tails = [ref[0, HEAD_DIM : HEAD_DIM + LOCAL, :] for ref in refs]
    by_y = [sum(flag(where[i] == j) * tails[i] for i in range(4)) for j in range(4)]
    gain_ref[...] = ((by_y[0] + by_y[1]) + by_y[2]) + by_y[3]
    half_ref[...] = sum(ref[:, 0:HEAD_DIM, :] for ref in refs)


def final_kernel(
    k_ref, v_ref, cols_ref, half_ref, other_ref, zeroth_ref, first_ref, grad_k_ref, grad_v_ref, out_k_ref, out_v_ref
):
    core = place()[2]
    even = core == 0
    for head in range(LOCAL):
        slot = head % 2
        half = jnp.where(core == head // 2, half_ref[slot], other_ref[slot])
        carry = jnp.exp(first_ref[0, HEAD_DIM + 4 + head : HEAD_DIM + 5 + head, :])
        high, low = split(jnp.where(even, carry * half + zeroth_ref[head], half))
        tail = cols_ref[:, 24 + head : 25 + head]
        k, v = k_ref[head], v_ref[head]
        out_k_ref[head] = (grad_k_ref[head] + tail * (dot(v, high, NT) + dot(v, low, NT))).astype(BF16)
        out_v_ref[head] = (grad_v_ref[head] + tail * (dot(k, high, NN) + dot(k, low, NN))).astype(BF16)


def call(kernel, outs, *args, scratch=(), flops=0, hbm=(), limit=12):
    size = sum(a.size * a.dtype.itemsize for a in args)
    shapes = [jax.ShapeDtypeStruct(shape, kind) for shape, kind in outs]
    size += sum(s.size * s.dtype.itemsize for s in shapes)
    spaces = [pltpu.HBM if i in hbm else pltpu.VMEM for i in range(len(args))]
    return pl.pallas_call(
        kernel,
        out_shape=shapes,
        in_specs=[pl.BlockSpec(memory_space=space) for space in spaces],
        scratch_shapes=list(scratch),
        cost_estimate=pl.CostEstimate(flops=flops, bytes_accessed=size, transcendentals=0),
        compiler_params=pltpu.CompilerParams(vmem_limit_bytes=limit * 2**20),
    )(*args)


def layer(queries, keys, values, log_decay, level_weight, gate_input, norm_gain, out_grad):
    level_rows = jnp.transpose(level_weight, (1, 0, 2))
    message = ((2, ROWS, HEAD_DIM), F32)
    double = ((2, 2, ROWS, HEAD_DIM), F32)
    tokens = (LOCAL, WIDTH, HEAD_DIM)
    square = (LOCAL, WIDTH, WIDTH)
    info = ((2, 8, HEAD_DIM), F32)
    columns = ((WIDTH, HEAD_DIM), F32)

    keep, away, running = call(
        state_kernel,
        [message, message, ((LOCAL, WIDTH), F32)],
        log_decay, keys, values,
        scratch=[pltpu.VMEM(tokens, BF16), pltpu.VMEM(tokens, BF16), pltpu.VMEM((16, WIDTH), F32), pltpu.SemaphoreType.DMA((2,))],
        hbm=(1, 2),
    )
    first = send(away, SWAP)
    (chip,) = call(pair_kernel, [message], keep, first)
    from_y = [send(chip, along_y(step)) for step in (1, 2, 3)]
    rest = send(keep, UP)
    inner, mixing, weight, scored, cols = call(
        intra_kernel,
        [(tokens, F32), (square, BF16), (square, F32), (square, F32), columns],
        queries, keys, values, level_rows, running,
        scratch=[pltpu.VMEM((HEAD_DIM, WIDTH), F32)],
        flops=10**9,
    )
    row, near, totals_y = call(y_kernel, [message, double, info], chip, *from_y)
    from_x = [send(row, along_x(step)) for step in (1, 2, 3)]
    near_other = send(near, SWAP)
    far, totals_x = call(x_kernel, [double, info], row, *from_x, totals_y)
    far_other = send(far, SWAP)
    bucket_kind = ((LOCAL, HEAD_DIM, INTER * HEAD_DIM), BF16)
    mixed, pay, bucket, finer, shift = call(
        mixed_kernel,
        [(tokens, F32), ((8, 4, HEAD_DIM), F32), bucket_kind, bucket_kind, ((LOCAL, 8, HEAD_DIM), F32)],
        queries, inner, gate_input, out_grad, norm_gain, cols, near, near_other, far, far_other, first, rest,
    )
    sums = lax.all_to_all(pay, "head", 0, 0, tiled=True)
    grad_mixed, scale, far_keep, far_away = call(
        gate_kernel,
        [(tokens, BF16), ((2, WIDTH, HEAD_DIM), F32), double, double],
        queries, mixed, gate_input, out_grad, norm_gain, cols, shift, sums,
    )
    to_one, to_far = call(meet_kernel, [message] * 2, far_keep, send(far_away, SWAP))
    back_x = [send(to_one, along_x(-1)), send(to_far, along_x(-2)), send(to_far, along_x(-3))]
    layer_out, grad_gate, near_keep, near_away, zeroth = call(
        close_kernel,
        [(tokens, BF16)] * 2 + [double] * 2 + [((LOCAL, HEAD_DIM, HEAD_DIM), F32)],
        queries, grad_mixed, mixed, gate_input, out_grad, norm_gain, cols, shift, scale,
        flops=10**9,
    )
    near_back = send(near_away, SWAP)
    messages = call(down_kernel, [message] * 4, to_far, *back_x, near_keep, near_back, totals_y, totals_x)
    back_y = [messages[0]] + [send(messages[step], along_y(-step)) for step in (1, 2, 3)]
    zeroth_back = send(zeroth, DOWN)
    grad_queries, grad_k, grad_v, levels = call(
        backward_kernel,
        [(tokens, BF16), (tokens, F32), (tokens, F32), ((LEVELS, LOCAL, WIDTH), F32)],
        queries, keys, values, grad_mixed, mixing, weight, scored, bucket, finer, cols, running,
        flops=10**9,
    )
    half, grad_gain = call(join_kernel, [((2, HEAD_DIM, HEAD_DIM), F32), ((LOCAL, HEAD_DIM), F32)], *back_y)
    half_other = send(half, SWAP)
    grad_keys, grad_values = call(
        final_kernel,
        [(tokens, BF16)] * 2,
        keys, values, cols, half, half_other, zeroth_back, first, grad_k, grad_v,
    )
    grad_levels = jnp.transpose(levels, (1, 0, 2))
    return (layer_out, grad_queries, grad_keys, grad_values, grad_levels, grad_gate, grad_gain)


def solution(mesh):
    rows = P("head", "seq", None)
    in_specs = (rows, rows, rows, P("head", "seq"), P("head", None, "seq"), rows, P("head", None), rows)
    out_specs = (rows, rows, rows, rows, P("head", None, "seq"), rows, P("head", None))
    return jax.shard_map(layer, mesh=mesh, in_specs=in_specs, out_specs=out_specs, check_vma=False)
```

```python
import jax
import jax.numpy as jnp
from jax import lax
from jax.experimental import pallas as pl
from jax.experimental.pallas import tpu as pltpu
from jax.sharding import PartitionSpec as P


HEADS = 32
HEAD_DIM = 128
TOTAL = HEADS * HEAD_DIM
EPSILON = 1e-05
HIGH = lax.Precision.HIGHEST
F32 = jnp.float32
BF16 = jnp.bfloat16

LOCAL = 4
WIDTH = 256
DEPTH = 8
INTER = 5
LEVELS = 21
ROWS = HEAD_DIM + 8


def place():
    me = lax.axis_index("seq")
    return me // 8, lax.rem(me // 2, 4), lax.rem(me, 2)


def ring(function):
    pairs = []
    for x in range(4):
        for y in range(4):
            for core in range(2):
                to = function(x, y, core)
                if to is not None:
                    pairs.append(((x * 4 + y) * 2 + core, (to[0] * 4 + to[1]) * 2 + to[2]))
    return pairs


SWAP = ring(lambda x, y, core: (x, y, 1 - core))
UP = ring(lambda x, y, core: (x, y, 1) if core == 0 else None)
DOWN = ring(lambda x, y, core: (x, y, 0) if core == 1 else None)


Z_STEPS = (((0, 1), (2, 3), (4, 5), (6, 7)), ((1, 2), (3, 4), (5, 6), (7, 0)), ((0, 3), (1, 6), (2, 5), (4, 7)))


def along_z(array, step):
    pairs = [pair for a, b in Z_STEPS[step] for pair in ((a, b), (b, a))]
    return lax.ppermute(array, "head", pairs)


def along_y(step):
    return ring(lambda x, y, core: (x, (y + step) % 4, core))


def along_x(step):
    return ring(lambda x, y, core: ((x + step) % 4, y, core))


def send(array, pairs):
    return lax.ppermute(array, "seq", pairs)


def split(array):
    high = array.astype(BF16)
    return high, (array - high.astype(F32)).astype(BF16)


def flag(condition):
    return condition.astype(F32)


def dot(a, b, dims, precision=None):
    return lax.dot_general(a, b, (dims, ((), ())), precision=precision, preferred_element_type=F32)


NN = ((1,), (0,))
NT = ((1,), (1,))
TN = ((0,), (0,))


def iotas(shape):
    return lax.broadcasted_iota(jnp.int32, shape, 0), lax.broadcasted_iota(jnp.int32, shape, 1)


def state_kernel(
    decay_hbm, k_hbm, v_hbm, keep_ref, send_ref, run_ref, decay_ref, k_ref, v_ref, rows_ref, sems
):
    copies = [
        pltpu.make_async_copy(source, to, sems.at[i])
        for i, (source, to) in enumerate(((decay_hbm, decay_ref), (v_hbm, v_ref), (k_hbm, k_ref)))
    ]
    for copy in copies:
        copy.start()
    core = place()[2]
    early, late = iotas((WIDTH, WIDTH))
    upper = (early <= late).astype(F32).astype(BF16)
    copies[0].wait()
    decay = decay_ref[...]
    first = decay.astype(BF16).astype(F32)
    second = (decay - first).astype(BF16).astype(F32)
    rows_ref[0:4, :] = first
    rows_ref[4:8, :] = second
    rows_ref[8:12, :] = decay - first - second
    rows_ref[12:16, :] = jnp.zeros((4, WIDTH), F32)
    parts = dot(rows_ref[...].astype(BF16), upper, NN)
    running = parts[0:4, :] + parts[4:8, :] + parts[8:12, :]
    run_ref[...] = running
    rows_ref[0:4, :] = jnp.exp(running[:, WIDTH - 1 :] - running)
    tails = jnp.transpose(rows_ref[...])
    for copy in copies[1:]:
        copy.wait()
    for head in range(LOCAL):
        weighted = v_ref[head].astype(F32) * tails[:, head : head + 1]
        both = dot(k_ref[head], jnp.concatenate(split(weighted), axis=1), TN)
        state = both[:, 0:HEAD_DIM] + both[:, HEAD_DIM:]
        total = jnp.broadcast_to(running[head : head + 1, WIDTH - 1 :], (4, HEAD_DIM))
        totals = jnp.broadcast_to(running[:, WIDTH - 1 :], (4, HEAD_DIM))

        def put(ref):
            ref[head % 2, 0:HEAD_DIM, :] = state
            ref[head % 2, HEAD_DIM : HEAD_DIM + 4, :] = total
            ref[head % 2, HEAD_DIM + 4 :, :] = totals

        pl.when(core == head // 2)(lambda: put(keep_ref))
        pl.when(core != head // 2)(lambda: put(send_ref))


def pair_kernel(keep_ref, first_ref, chip_ref):
    late = place()[2] == 1
    before = jnp.where(late, first_ref[...], keep_ref[...])
    after = jnp.where(late, keep_ref[...], first_ref[...])
    carry = jnp.exp(after[:, HEAD_DIM : HEAD_DIM + 1, :])
    chip_ref[:, 0:HEAD_DIM, :] = carry * before[:, 0:HEAD_DIM, :] + after[:, 0:HEAD_DIM, :]
    chip_ref[:, HEAD_DIM:, :] = before[:, HEAD_DIM:, :] + after[:, HEAD_DIM:, :]


def intra_kernel(
    q_ref, k_ref, v_ref, level_ref, run_ref, inner_ref, mix_ref, weight_ref, scored_ref, cols_ref, rows_ref
):
    running = run_ref[...]
    grown = jnp.exp(running)
    rows_ref[...] = jnp.zeros_like(rows_ref)
    for level in range(INTER):
        rows_ref[4 * level : 4 * level + 4, :] = level_ref[DEPTH + 1 + level] * grown
    rows_ref[20:24, :] = running
    rows_ref[24:28, :] = jnp.exp(running[:, WIDTH - 1 :] - running)
    cols_ref[...] = jnp.transpose(rows_ref[...])
    early, late = iotas((WIDTH, WIDTH))
    crossed = jnp.bitwise_xor(early, late)
    causal = early <= late
    for head in range(LOCAL):
        spread = run_ref[head : head + 1, :] - cols_ref[:, 20 + head : 21 + head]
        decay = jnp.where(causal, jnp.exp(jnp.where(causal, spread, 0.0)), 0.0)
        chosen = jnp.broadcast_to(level_ref[0, head : head + 1, :], (WIDTH, WIDTH))
        for level in range(1, DEPTH + 1):
            chosen = jnp.where(crossed >= 2 ** (level - 1), level_ref[level, head : head + 1, :], chosen)
        scored = dot(k_ref[head], q_ref[head], NT)
        weight = decay * chosen
        mixing = (scored * weight).astype(BF16)
        weight_ref[head] = weight
        scored_ref[head] = scored * decay
        mix_ref[head] = mixing
        inner_ref[head] = dot(mixing, v_ref[head], TN)


def order(position, step):
    return lax.rem(position + 4 - step, 4)


def y_kernel(own_ref, one_ref, two_ref, three_ref, next_ref, bucket_ref, info_ref):
    y = place()[1]
    refs = (own_ref, one_ref, two_ref, three_ref)
    where = [order(y, step) for step in range(4)]
    totals = [ref[:, HEAD_DIM : HEAD_DIM + 1, :] for ref in refs]
    by_y = [sum(flag(where[i] == j) * totals[i] for i in range(4)) for j in range(4)]
    carry = jnp.exp(by_y[1])
    whole = jnp.zeros((2, HEAD_DIM, HEAD_DIM), F32)
    pair = jnp.zeros((2, HEAD_DIM, HEAD_DIM), F32)
    for i in range(4):
        state = refs[i][:, 0:HEAD_DIM, :]
        later = sum(flag(j > where[i]) * by_y[j] for j in range(1, 4))
        whole = whole + jnp.exp(later) * state
        if i:
            part = flag(y >= 2) * (flag(where[i] == 1) + flag(where[i] == 0) * carry)
            pair = pair + part * state
    below = sum(flag(j < y) * by_y[j] for j in range(3))
    next_ref[:, 0:HEAD_DIM, :] = whole
    next_ref[:, HEAD_DIM:, :] = jnp.broadcast_to(by_y[0] + by_y[1] + by_y[2] + by_y[3], (2, 8, HEAD_DIM))
    bucket_ref[0, :, 0:HEAD_DIM, :] = flag(lax.rem(y, 2) == 1) * one_ref[:, 0:HEAD_DIM, :]
    bucket_ref[0, :, HEAD_DIM:, :] = jnp.zeros((2, 8, HEAD_DIM), F32)
    bucket_ref[1, :, 0:HEAD_DIM, :] = pair
    bucket_ref[1, :, HEAD_DIM:, :] = jnp.broadcast_to(flag(y == 3) * by_y[2], (2, 8, HEAD_DIM))
    for j in range(4):
        info_ref[:, j : j + 1, :] = by_y[j]
    info_ref[:, 4:8, :] = jnp.broadcast_to(below, (2, 4, HEAD_DIM))


def x_kernel(own_ref, one_ref, two_ref, three_ref, info_ref, bucket_ref, wide_ref):
    x = place()[0]
    refs = (own_ref, one_ref, two_ref, three_ref)
    where = [order(x, step) for step in range(4)]
    totals = [ref[:, HEAD_DIM : HEAD_DIM + 1, :] for ref in refs]
    by_x = [sum(flag(where[i] == j) * totals[i] for i in range(4)) for j in range(4)]
    carry = jnp.exp(by_x[1])
    pair = jnp.zeros((2, HEAD_DIM, HEAD_DIM), F32)
    for i in range(1, 4):
        part = flag(x >= 2) * (flag(where[i] == 1) + flag(where[i] == 0) * carry)
        pair = pair + part * refs[i][:, 0:HEAD_DIM, :]
    below = info_ref[:, 4:5, :]
    bucket_ref[0, :, 0:HEAD_DIM, :] = flag(lax.rem(x, 2) == 1) * one_ref[:, 0:HEAD_DIM, :]
    bucket_ref[0, :, HEAD_DIM:, :] = jnp.broadcast_to(below, (2, 8, HEAD_DIM))
    bucket_ref[1, :, 0:HEAD_DIM, :] = pair
    bucket_ref[1, :, HEAD_DIM:, :] = jnp.broadcast_to(below + flag(x == 3) * by_x[2], (2, 8, HEAD_DIM))
    for j in range(4):
        wide_ref[:, j : j + 1, :] = by_x[j]
        wide_ref[:, 4 + j : 5 + j, :] = by_x[j]


def mixed_kernel(
    q_ref, inner_ref, gate_ref, grad_ref, gain_ref, cols_ref, near_ref, near_other_ref, far_ref, far_other_ref,
    first_ref, rest_ref, mixed_ref, pay_ref, bucket_ref, finer_ref, shift_ref,
):
    core = place()[2]
    odd = flag(core == 1)
    ones = jnp.ones((8, HEAD_DIM), BF16)
    squares = jnp.zeros((8, WIDTH), F32)
    crosses = jnp.zeros((8, WIDTH), F32)
    for head in range(LOCAL):
        slot, mine = head % 2, core == head // 2
        zeroth = rest_ref[slot, 0:HEAD_DIM, :] if head < 2 else first_ref[slot, 0:HEAD_DIM, :]
        earlier = odd * first_ref[0, HEAD_DIM + 4 + head : HEAD_DIM + 5 + head, :]
        parts = [split(odd * zeroth)]
        shift_ref[head] = jnp.ones((8, HEAD_DIM), F32)
        for level in range(1, INTER):
            own, other = (near_ref, near_other_ref) if level < 3 else (far_ref, far_other_ref)
            at = (level - 1) % 2
            chosen = jnp.where(mine, own[at, slot], other[at, slot])
            shift = jnp.exp(earlier + chosen[HEAD_DIM : HEAD_DIM + 1, :])
            shift_ref[head, level : level + 1, :] = shift
            parts.append(split(chosen[0:HEAD_DIM, :] * shift))
        bucket, finer = (jnp.concatenate([part[i] for part in parts], axis=1) for i in range(2))
        bucket_ref[head] = bucket
        finer_ref[head] = finer
        through = dot(q_ref[head], bucket, NN) + dot(q_ref[head], finer, NN)
        mixed = inner_ref[head]
        for level in range(INTER):
            at = 4 * level + head
            mixed = mixed + cols_ref[:, at : at + 1] * through[:, HEAD_DIM * level : HEAD_DIM * (level + 1)]
        mixed_ref[head] = mixed
        gate = gate_ref[head].astype(F32)
        gated = mixed * (gate * jax.nn.sigmoid(gate))
        scaled = grad_ref[head].astype(F32) * gain_ref[head : head + 1, :]
        squares = squares + dot(ones, (gated * gated).astype(BF16), NT)
        crosses = crosses + dot(ones, (gated * scaled).astype(BF16), NT)
    for half in range(2):
        piece = slice(HEAD_DIM * half, HEAD_DIM * (half + 1))
        pay_ref[half : half + 1, :] = squares[0:1, piece]
        pay_ref[2 + half : 3 + half, :] = crosses[0:1, piece]
    pay_ref[4:8, :] = jnp.zeros((4, HEAD_DIM), F32)


def add_kernel(a_ref, b_ref, out_ref):
    out_ref[...] = a_ref[...] + b_ref[...]


def gate_kernel(
    q_ref, mixed_ref, gate_ref, grad_ref, gain_ref, cols_ref, shift_ref, sums_ref, other_ref,
    g_ref, scale_ref, keep_ref, send_ref,
):
    x, _, core = place()
    ones = jnp.ones((8, HEAD_DIM), F32)
    sums = sums_ref[...] + other_ref[...]
    row = iotas((8, HEAD_DIM))[0]
    wide = [dot(jnp.where(row == i, sums, 0.0), ones, TN, HIGH) for i in range(4)]
    squares = jnp.concatenate(wide[0:2], axis=0)
    crosses = jnp.concatenate(wide[2:4], axis=0)
    inverse = lax.rsqrt(squares * (1.0 / TOTAL) + EPSILON)
    pull = inverse * inverse * inverse * crosses * (1.0 / TOTAL)
    scale_ref[0] = inverse
    scale_ref[1] = pull
    gains = []
    for ref in (keep_ref, send_ref):
        ref[:, :, HEAD_DIM:, :] = jnp.zeros((2, 2, 8, HEAD_DIM), F32)
    for head in range(LOCAL):
        gate = gate_ref[head].astype(F32)
        act = gate * jax.nn.sigmoid(gate)
        gated = mixed_ref[head] * act
        grad = grad_ref[head].astype(F32)
        gains.append(jnp.sum(grad * (gated * inverse), axis=0, keepdims=True))
        grad_gated = inverse * (grad * gain_ref[head : head + 1, :]) - gated * pull
        g = (grad_gated * act).astype(BF16)
        g_ref[head] = g
        far = reached(q_ref[head], g.astype(F32), cols_ref, shift_ref, head, (3, 4))
        near = jnp.where(lax.rem(x, 2) == 1, far[0], far[1])

        def put(ref):
            ref[0, head % 2, 0:HEAD_DIM, :] = near
            ref[1, head % 2, 0:HEAD_DIM, :] = far[1]

        pl.when(core == head // 2)(lambda: put(keep_ref))
        pl.when(core != head // 2)(lambda: put(send_ref))
    for head in range(LOCAL):
        for ref in (keep_ref, send_ref):
            ref[0, 0, HEAD_DIM + head : HEAD_DIM + head + 1, :] = gains[head]
            ref[1, 0, HEAD_DIM + head : HEAD_DIM + head + 1, :] = gains[head]


def reached(q, g, cols_ref, shift_ref, head, levels):
    parts = [split(cols_ref[:, 4 * level + head : 4 * level + head + 1] * g) for level in levels]
    both = dot(q, jnp.concatenate([part for pair in parts for part in pair], axis=1), TN)
    found = []
    for i, level in enumerate(levels):
        at = 2 * HEAD_DIM * i
        grad = both[:, at : at + HEAD_DIM] + both[:, at + HEAD_DIM : at + 2 * HEAD_DIM]
        found.append(grad * shift_ref[head, level : level + 1, :])
    return found


def meet_kernel(keep_ref, other_ref, near_ref, far_ref):
    near_ref[...] = keep_ref[0] + other_ref[0]
    far_ref[...] = keep_ref[1] + other_ref[1]


def close_kernel(
    q_ref, g_ref, mixed_ref, gate_ref, grad_ref, gain_ref, cols_ref, shift_ref, scale_ref,
    out_ref, grad_gate_ref, keep_ref, send_ref, zeroth_ref,
):
    core = place()[2]
    inverse, pull = scale_ref[0], scale_ref[1]
    for ref in (keep_ref, send_ref):
        ref[:, :, HEAD_DIM:, :] = jnp.zeros((2, 2, 8, HEAD_DIM), F32)
    for head in range(LOCAL):
        near = reached(q_ref[head], g_ref[head].astype(F32), cols_ref, shift_ref, head, (0, 1, 2))
        zeroth_ref[head] = near[0]

        def put(ref):
            ref[0, head % 2, 0:HEAD_DIM, :] = near[1]
            ref[1, head % 2, 0:HEAD_DIM, :] = near[2]

        pl.when(core == head // 2)(lambda: put(keep_ref))
        pl.when(core != head // 2)(lambda: put(send_ref))
    for head in range(LOCAL):
        gain = gain_ref[head : head + 1, :]
        gate = gate_ref[head].astype(F32)
        sigmoid = jax.nn.sigmoid(gate)
        mixed = mixed_ref[head]
        gated = mixed * (gate * sigmoid)
        out_ref[head] = (gain * (gated * inverse)).astype(BF16)
        grad_gated = inverse * (grad_ref[head].astype(F32) * gain) - gated * pull
        grad_gate_ref[head] = (grad_gated * mixed * sigmoid * (1.0 + gate * (1.0 - sigmoid))).astype(BF16)


def down_kernel(
    own_ref, one_ref, two_ref, three_ref, near_ref, near_other_ref, info_ref, wide_ref,
    m0_ref, m1_ref, m2_ref, m3_ref,
):
    x, y, _ = place()
    refs = (own_ref, one_ref, two_ref, three_ref)
    carry_x = jnp.exp(wide_ref[:, 1:2, :])
    first = x == 0
    c1 = flag(x <= 2)
    c2 = flag(first) * carry_x + flag(x == 1)
    c3 = flag(first) * carry_x
    body = slice(0, HEAD_DIM)
    state = c1 * one_ref[:, body, :] + c2 * two_ref[:, body, :] + c3 * three_ref[:, body, :]
    tails = [ref[:, HEAD_DIM:, :] for ref in refs]
    where = [lax.rem(x + step, 4) for step in range(4)]
    by_x = [sum(flag(where[i] == j) * tails[i] for i in range(4)) for j in range(4)]
    gains = ((by_x[0] + by_x[1]) + by_x[2]) + by_x[3]
    low = near_ref[0, :, body, :] + near_other_ref[0, :, body, :]
    high = near_ref[1, :, body, :] + near_other_ref[1, :, body, :]
    totals = [info_ref[:, j : j + 1, :] for j in range(4)]
    after = [totals[1] + totals[2] + totals[3], totals[2] + totals[3], totals[3], jnp.zeros_like(totals[3])]
    after = [jnp.exp(part) for part in after]
    carry_y = jnp.exp(totals[1])
    for step, ref in enumerate((m0_ref, m1_ref, m2_ref, m3_ref)):
        to = order(y, step)
        message = sum(flag(to == j) * after[j] for j in range(4)) * state
        if step == 1:
            message = message + flag(lax.rem(y, 2) == 1) * low
        if step:
            message = message + flag(y >= 2) * (flag(to == 1) + flag(to == 0) * carry_y) * high
        ref[:, body, :] = message
        ref[:, HEAD_DIM:, :] = gains


def backward_kernel(
    q_ref, k_ref, v_ref, g_ref, mix_ref, weight_ref, scored_ref, bucket_ref, finer_ref, cols_ref, run_ref,
    grad_q_ref, grad_k_ref, grad_v_ref, levels_ref,
):
    early, late = iotas((WIDTH, WIDTH))
    crossed = jnp.bitwise_xor(early, late)
    ones = jnp.ones((8, HEAD_DIM), BF16)
    for level in range(DEPTH + 1 + INTER, LEVELS):
        levels_ref[level] = jnp.zeros((LOCAL, WIDTH), F32)
    for head in range(LOCAL):
        q, k, v, g = q_ref[head], k_ref[head], v_ref[head], g_ref[head]
        grad_mixing = dot(v, g, NT)
        grad_scores = (grad_mixing * weight_ref[head]).astype(BF16)
        grad_k_ref[head] = dot(grad_scores, q, NN)
        grad_v_ref[head] = dot(mix_ref[head], g, NN)
        grad_q = dot(grad_scores, k, TN)
        moved = grad_mixing * scored_ref[head]
        for level in range(DEPTH + 1):
            inside = crossed == 0
            if level:
                inside = (crossed >= 2 ** (level - 1)) & (crossed < 2**level)
            levels_ref[level, head : head + 1, :] = jnp.sum(jnp.where(inside, moved, 0.0), axis=0, keepdims=True)
        wide_q = q.astype(F32)
        grown = jnp.exp(run_ref[head : head + 1, :])
        for level in range(INTER):
            piece = slice(HEAD_DIM * level, HEAD_DIM * (level + 1))
            pulled = dot(g, bucket_ref[head, :, piece], NT) + dot(g, finer_ref[head, :, piece], NT)
            at = 4 * level + head
            grad_q = grad_q + cols_ref[:, at : at + 1] * pulled
            high, low = split(wide_q * pulled)
            sums = dot(ones, high, NT) + dot(ones, low, NT)
            levels_ref[DEPTH + 1 + level, head : head + 1, :] = grown * sums[0:1, :]
        grad_q_ref[head] = grad_q.astype(BF16)


def join_kernel(own_ref, one_ref, two_ref, three_ref, half_ref, sum_ref):
    y = place()[1]
    refs = (own_ref, one_ref, two_ref, three_ref)
    where = [lax.rem(y + step, 4) for step in range(4)]
    tails = [ref[0, HEAD_DIM : HEAD_DIM + LOCAL, :] for ref in refs]
    by_y = [sum(flag(where[i] == j) * tails[i] for i in range(4)) for j in range(4)]
    sum_ref[...] = ((by_y[0] + by_y[1]) + by_y[2]) + by_y[3]
    half_ref[...] = sum(ref[:, 0:HEAD_DIM, :] for ref in refs)


def final_kernel(
    k_ref, v_ref, cols_ref, half_ref, other_ref, zeroth_ref, first_ref, grad_k_ref, grad_v_ref, sum_ref,
    out_k_ref, out_v_ref, gain_ref,
):
    gain_ref[...] = sum_ref[...]
    core = place()[2]
    even = core == 0
    for head in range(LOCAL):
        slot = head % 2
        half = jnp.where(core == head // 2, half_ref[slot], other_ref[slot])
        carry = jnp.exp(first_ref[0, HEAD_DIM + 4 + head : HEAD_DIM + 5 + head, :])
        high, low = split(jnp.where(even, carry * half + zeroth_ref[head], half))
        tail = cols_ref[:, 24 + head : 25 + head]
        k, v = k_ref[head], v_ref[head]
        out_k_ref[head] = (grad_k_ref[head] + tail * (dot(v, high, NT) + dot(v, low, NT))).astype(BF16)
        out_v_ref[head] = (grad_v_ref[head] + tail * (dot(k, high, NN) + dot(k, low, NN))).astype(BF16)


def call(kernel, outs, *args, scratch=(), flops=0, hbm=(), limit=12):
    size = sum(a.size * a.dtype.itemsize for a in args)
    shapes = [jax.ShapeDtypeStruct(shape, kind) for shape, kind in outs]
    size += sum(s.size * s.dtype.itemsize for s in shapes)
    spaces = [pltpu.HBM if i in hbm else pltpu.VMEM for i in range(len(args))]
    return pl.pallas_call(
        kernel,
        out_shape=shapes,
        in_specs=[pl.BlockSpec(memory_space=space) for space in spaces],
        scratch_shapes=list(scratch),
        cost_estimate=pl.CostEstimate(flops=flops, bytes_accessed=size, transcendentals=0),
        compiler_params=pltpu.CompilerParams(vmem_limit_bytes=limit * 2**20),
    )(*args)


def layer(queries, keys, values, log_decay, level_weight, gate_input, norm_gain, out_grad):
    level_rows = jnp.transpose(level_weight, (1, 0, 2))
    message = ((2, ROWS, HEAD_DIM), F32)
    double = ((2, 2, ROWS, HEAD_DIM), F32)
    tokens = (LOCAL, WIDTH, HEAD_DIM)
    square = (LOCAL, WIDTH, WIDTH)
    info = ((2, 8, HEAD_DIM), F32)
    columns = ((WIDTH, HEAD_DIM), F32)

    keep, away, running = call(
        state_kernel,
        [message, message, ((LOCAL, WIDTH), F32)],
        *(pltpu.with_memory_space_constraint(a, pltpu.HBM) for a in (log_decay, keys, values)),
        scratch=[
            pltpu.VMEM((LOCAL, WIDTH), F32), pltpu.VMEM(tokens, BF16), pltpu.VMEM(tokens, BF16),
            pltpu.VMEM((16, WIDTH), F32), pltpu.SemaphoreType.DMA((3,)),
        ],
        hbm=(0, 1, 2),
    )
    first = send(away, SWAP)
    (chip,) = call(pair_kernel, [message], keep, first)
    from_y = [send(chip, along_y(step)) for step in (1, 2, 3)]
    rest = send(keep, UP)
    inner, mixing, weight, scored, cols = call(
        intra_kernel,
        [(tokens, F32), (square, BF16), (square, F32), (square, F32), columns],
        queries, keys, values, level_rows, running,
        scratch=[pltpu.VMEM((HEAD_DIM, WIDTH), F32)],
        flops=10**9,
    )
    row, near, totals_y = call(y_kernel, [message, double, info], chip, *from_y)
    from_x = [send(row, along_x(step)) for step in (1, 2, 3)]
    near_other = send(near, SWAP)
    far, totals_x = call(x_kernel, [double, info], row, *from_x, totals_y)
    far_other = send(far, SWAP)
    bucket_kind = ((LOCAL, HEAD_DIM, INTER * HEAD_DIM), BF16)
    mixed, pay, bucket, finer, shift = call(
        mixed_kernel,
        [(tokens, F32), ((8, HEAD_DIM), F32), bucket_kind, bucket_kind, ((LOCAL, 8, HEAD_DIM), F32)],
        queries, inner, gate_input, out_grad, norm_gain, cols, near, near_other, far, far_other, first, rest,
    )
    for step in range(2):
        (pay,) = call(add_kernel, [((8, HEAD_DIM), F32)], pay, along_z(pay, step))
    grad_mixed, scale, far_keep, far_away = call(
        gate_kernel,
        [(tokens, BF16), ((2, WIDTH, HEAD_DIM), F32), double, double],
        queries, mixed, gate_input, out_grad, norm_gain, cols, shift, pay, along_z(pay, 2),
    )
    to_one, to_far = call(meet_kernel, [message] * 2, far_keep, send(far_away, SWAP))
    back_x = [send(to_one, along_x(-1)), send(to_far, along_x(-2)), send(to_far, along_x(-3))]
    layer_out, grad_gate, near_keep, near_away, zeroth = call(
        close_kernel,
        [(tokens, BF16)] * 2 + [double] * 2 + [((LOCAL, HEAD_DIM, HEAD_DIM), F32)],
        queries, grad_mixed, mixed, gate_input, out_grad, norm_gain, cols, shift, scale,
        flops=10**9,
    )
    near_back = send(near_away, SWAP)
    messages = call(down_kernel, [message] * 4, to_far, *back_x, near_keep, near_back, totals_y, totals_x)
    back_y = [messages[0]] + [send(messages[step], along_y(-step)) for step in (1, 2, 3)]
    zeroth_back = send(zeroth, DOWN)
    grad_queries, grad_k, grad_v, levels = call(
        backward_kernel,
        [(tokens, BF16), (tokens, F32), (tokens, F32), ((LEVELS, LOCAL, WIDTH), F32)],
        queries, keys, values, grad_mixed, mixing, weight, scored, bucket, finer, cols, running,
        flops=10**9,
    )
    half, gain_sum = call(join_kernel, [((2, HEAD_DIM, HEAD_DIM), F32), ((LOCAL, HEAD_DIM), F32)], *back_y)
    half_other = send(half, SWAP)
    grad_keys, grad_values, grad_gain = call(
        final_kernel,
        [(tokens, BF16)] * 2 + [((LOCAL, HEAD_DIM), F32)],
        keys, values, cols, half, half_other, zeroth_back, first, grad_k, grad_v, gain_sum,
    )
    grad_levels = jnp.transpose(levels, (1, 0, 2))
    return (layer_out, grad_queries, grad_keys, grad_values, grad_levels, grad_gate, grad_gain)


def solution(mesh):
    rows = P("head", "seq", None)
    in_specs = (rows, rows, rows, P("head", "seq"), P("head", None, "seq"), rows, P("head", None), rows)
    out_specs = (rows, rows, rows, rows, P("head", None, "seq"), rows, P("head", None))
    return jax.shard_map(layer, mesh=mesh, in_specs=in_specs, out_specs=out_specs, check_vma=False)
```

```python
import jax
import jax.numpy as jnp
from jax import lax
from jax.experimental import pallas as pl
from jax.experimental.pallas import tpu as pltpu
from jax.sharding import PartitionSpec as P


HEADS = 32
HEAD_DIM = 128
TOTAL = HEADS * HEAD_DIM
EPSILON = 1e-05
HIGH = lax.Precision.HIGHEST
F32 = jnp.float32
BF16 = jnp.bfloat16

LOCAL = 4
WIDTH = 256
DEPTH = 8
INTER = 5
LEVELS = 21
ROWS = HEAD_DIM + 8


def place():
    me = lax.axis_index("seq")
    return me // 8, lax.rem(me // 2, 4), lax.rem(me, 2)


def ring(function):
    pairs = []
    for x in range(4):
        for y in range(4):
            for core in range(2):
                to = function(x, y, core)
                if to is not None:
                    pairs.append(((x * 4 + y) * 2 + core, (to[0] * 4 + to[1]) * 2 + to[2]))
    return pairs


SWAP = ring(lambda x, y, core: (x, y, 1 - core))
UP = ring(lambda x, y, core: (x, y, 1) if core == 0 else None)
DOWN = ring(lambda x, y, core: (x, y, 0) if core == 1 else None)


Z_PAIRS = ((0, 1), (2, 3), (4, 5), (6, 7))
Z_FAR = ((1, 4), (3, 6), (5, 0), (7, 2))
Z_NEXT = ((1, 2), (3, 4), (5, 6), (7, 0))
Z_TWO = [(z, (z + 6 + 4 * (z % 2)) % 8) for z in range(8)]


def both_ways(pairs):
    return [pair for a, b in pairs for pair in ((a, b), (b, a))]


def along_z(array, pairs):
    return lax.ppermute(array, "head", pairs)


def along_y(step):
    return ring(lambda x, y, core: (x, (y + step) % 4, core))


def along_x(step):
    return ring(lambda x, y, core: ((x + step) % 4, y, core))


def send(array, pairs):
    return lax.ppermute(array, "seq", pairs)


def split(array):
    high = array.astype(BF16)
    return high, (array - high.astype(F32)).astype(BF16)


def flag(condition):
    return condition.astype(F32)


def dot(a, b, dims, precision=None):
    return lax.dot_general(a, b, (dims, ((), ())), precision=precision, preferred_element_type=F32)


NN = ((1,), (0,))
NT = ((1,), (1,))
TN = ((0,), (0,))


def iotas(shape):
    return lax.broadcasted_iota(jnp.int32, shape, 0), lax.broadcasted_iota(jnp.int32, shape, 1)


def state_kernel(
    decay_hbm, k_hbm, v_hbm, keep_ref, send_ref, run_ref, decay_ref, k_ref, v_ref, rows_ref, sems
):
    copies = [
        pltpu.make_async_copy(source, to, sems.at[i])
        for i, (source, to) in enumerate(((decay_hbm, decay_ref), (v_hbm, v_ref), (k_hbm, k_ref)))
    ]
    for copy in copies:
        copy.start()
    core = place()[2]
    early, late = iotas((WIDTH, WIDTH))
    upper = (early <= late).astype(F32).astype(BF16)
    copies[0].wait()
    decay = decay_ref[...]
    first = decay.astype(BF16).astype(F32)
    second = (decay - first).astype(BF16).astype(F32)
    rows_ref[0:4, :] = first
    rows_ref[4:8, :] = second
    rows_ref[8:12, :] = decay - first - second
    rows_ref[12:16, :] = jnp.zeros((4, WIDTH), F32)
    parts = dot(rows_ref[...].astype(BF16), upper, NN)
    running = parts[0:4, :] + parts[4:8, :] + parts[8:12, :]
    run_ref[...] = running
    rows_ref[0:4, :] = jnp.exp(running[:, WIDTH - 1 :] - running)
    tails = jnp.transpose(rows_ref[...])
    for copy in copies[1:]:
        copy.wait()
    for head in range(LOCAL):
        weighted = v_ref[head].astype(F32) * tails[:, head : head + 1]
        both = dot(k_ref[head], jnp.concatenate(split(weighted), axis=1), TN)
        state = both[:, 0:HEAD_DIM] + both[:, HEAD_DIM:]
        total = jnp.broadcast_to(running[head : head + 1, WIDTH - 1 :], (4, HEAD_DIM))
        totals = jnp.broadcast_to(running[:, WIDTH - 1 :], (4, HEAD_DIM))

        def put(ref):
            ref[head % 2, 0:HEAD_DIM, :] = state
            ref[head % 2, HEAD_DIM : HEAD_DIM + 4, :] = total
            ref[head % 2, HEAD_DIM + 4 :, :] = totals

        pl.when(core == head // 2)(lambda: put(keep_ref))
        pl.when(core != head // 2)(lambda: put(send_ref))


def pair_kernel(keep_ref, first_ref, chip_ref):
    late = place()[2] == 1
    before = jnp.where(late, first_ref[...], keep_ref[...])
    after = jnp.where(late, keep_ref[...], first_ref[...])
    carry = jnp.exp(after[:, HEAD_DIM : HEAD_DIM + 1, :])
    chip_ref[:, 0:HEAD_DIM, :] = carry * before[:, 0:HEAD_DIM, :] + after[:, 0:HEAD_DIM, :]
    chip_ref[:, HEAD_DIM:, :] = before[:, HEAD_DIM:, :] + after[:, HEAD_DIM:, :]


def intra_kernel(
    q_ref, k_ref, v_ref, level_ref, run_ref, inner_ref, mix_ref, weight_ref, scored_ref, cols_ref, rows_ref
):
    running = run_ref[...]
    grown = jnp.exp(running)
    rows_ref[...] = jnp.zeros_like(rows_ref)
    for level in range(INTER):
        rows_ref[4 * level : 4 * level + 4, :] = level_ref[DEPTH + 1 + level] * grown
    rows_ref[20:24, :] = running
    rows_ref[24:28, :] = jnp.exp(running[:, WIDTH - 1 :] - running)
    cols_ref[...] = jnp.transpose(rows_ref[...])
    early, late = iotas((WIDTH, WIDTH))
    crossed = jnp.bitwise_xor(early, late)
    causal = early <= late
    for head in range(LOCAL):
        spread = run_ref[head : head + 1, :] - cols_ref[:, 20 + head : 21 + head]
        decay = jnp.where(causal, jnp.exp(jnp.where(causal, spread, 0.0)), 0.0)
        chosen = jnp.broadcast_to(level_ref[0, head : head + 1, :], (WIDTH, WIDTH))
        for level in range(1, DEPTH + 1):
            chosen = jnp.where(crossed >= 2 ** (level - 1), level_ref[level, head : head + 1, :], chosen)
        scored = dot(k_ref[head], q_ref[head], NT)
        weight = decay * chosen
        mixing = (scored * weight).astype(BF16)
        weight_ref[head] = weight
        scored_ref[head] = scored * decay
        mix_ref[head] = mixing
        inner_ref[head] = dot(mixing, v_ref[head], TN)


def order(position, step):
    return lax.rem(position + 4 - step, 4)


def y_kernel(own_ref, one_ref, two_ref, three_ref, next_ref, bucket_ref, info_ref):
    y = place()[1]
    refs = (own_ref, one_ref, two_ref, three_ref)
    where = [order(y, step) for step in range(4)]
    totals = [ref[:, HEAD_DIM : HEAD_DIM + 1, :] for ref in refs]
    by_y = [sum(flag(where[i] == j) * totals[i] for i in range(4)) for j in range(4)]
    carry = jnp.exp(by_y[1])
    whole = jnp.zeros((2, HEAD_DIM, HEAD_DIM), F32)
    pair = jnp.zeros((2, HEAD_DIM, HEAD_DIM), F32)
    for i in range(4):
        state = refs[i][:, 0:HEAD_DIM, :]
        later = sum(flag(j > where[i]) * by_y[j] for j in range(1, 4))
        whole = whole + jnp.exp(later) * state
        if i:
            part = flag(y >= 2) * (flag(where[i] == 1) + flag(where[i] == 0) * carry)
            pair = pair + part * state
    below = sum(flag(j < y) * by_y[j] for j in range(3))
    next_ref[:, 0:HEAD_DIM, :] = whole
    next_ref[:, HEAD_DIM:, :] = jnp.broadcast_to(by_y[0] + by_y[1] + by_y[2] + by_y[3], (2, 8, HEAD_DIM))
    bucket_ref[0, :, 0:HEAD_DIM, :] = flag(lax.rem(y, 2) == 1) * one_ref[:, 0:HEAD_DIM, :]
    bucket_ref[0, :, HEAD_DIM:, :] = jnp.zeros((2, 8, HEAD_DIM), F32)
    bucket_ref[1, :, 0:HEAD_DIM, :] = pair
    bucket_ref[1, :, HEAD_DIM:, :] = jnp.broadcast_to(flag(y == 3) * by_y[2], (2, 8, HEAD_DIM))
    for j in range(4):
        info_ref[:, j : j + 1, :] = by_y[j]
    info_ref[:, 4:8, :] = jnp.broadcast_to(below, (2, 4, HEAD_DIM))


def x_kernel(own_ref, one_ref, two_ref, three_ref, info_ref, bucket_ref, wide_ref):
    x = place()[0]
    refs = (own_ref, one_ref, two_ref, three_ref)
    where = [order(x, step) for step in range(4)]
    totals = [ref[:, HEAD_DIM : HEAD_DIM + 1, :] for ref in refs]
    by_x = [sum(flag(where[i] == j) * totals[i] for i in range(4)) for j in range(4)]
    carry = jnp.exp(by_x[1])
    pair = jnp.zeros((2, HEAD_DIM, HEAD_DIM), F32)
    for i in range(1, 4):
        part = flag(x >= 2) * (flag(where[i] == 1) + flag(where[i] == 0) * carry)
        pair = pair + part * refs[i][:, 0:HEAD_DIM, :]
    below = info_ref[:, 4:5, :]
    bucket_ref[0, :, 0:HEAD_DIM, :] = flag(lax.rem(x, 2) == 1) * one_ref[:, 0:HEAD_DIM, :]
    bucket_ref[0, :, HEAD_DIM:, :] = jnp.broadcast_to(below, (2, 8, HEAD_DIM))
    bucket_ref[1, :, 0:HEAD_DIM, :] = pair
    bucket_ref[1, :, HEAD_DIM:, :] = jnp.broadcast_to(below + flag(x == 3) * by_x[2], (2, 8, HEAD_DIM))
    for j in range(4):
        wide_ref[:, j : j + 1, :] = by_x[j]
        wide_ref[:, 4 + j : 5 + j, :] = by_x[j]


def through(q, parts, cols_ref, head, levels):
    bucket, finer = (jnp.concatenate([part[i] for part in parts], axis=1) for i in range(2))
    found = dot(q, bucket, NN) + dot(q, finer, NN)
    outer = sum(
        cols_ref[:, 4 * level + head : 4 * level + head + 1] * found[:, HEAD_DIM * i : HEAD_DIM * (i + 1)]
        for i, level in enumerate(levels)
    )
    return bucket, finer, outer


def chosen_bucket(own_ref, other_ref, at, head, core):
    return jnp.where(core == head // 2, own_ref[at, head % 2], other_ref[at, head % 2])


def near_kernel(
    q_ref, inner_ref, gate_ref, grad_ref, gain_ref, cols_ref, own_ref, other_ref, first_ref, rest_ref,
    mixed_ref, act_ref, pulled_ref, bucket_ref, finer_ref, shift_ref, scaled_ref, turned_ref,
):
    core = place()[2]
    odd = flag(core == 1)
    for head in range(LOCAL):
        slot = head % 2
        zeroth = rest_ref[slot, 0:HEAD_DIM, :] if head < 2 else first_ref[slot, 0:HEAD_DIM, :]
        earlier = odd * first_ref[0, HEAD_DIM + 4 + head : HEAD_DIM + 5 + head, :]
        parts = [split(odd * zeroth)]
        shift_ref[head] = jnp.ones((8, HEAD_DIM), F32)
        shift_ref[head, 7:8, :] = earlier
        for level in (1, 2):
            chosen = chosen_bucket(own_ref, other_ref, level - 1, head, core)
            shift = jnp.exp(earlier + chosen[HEAD_DIM : HEAD_DIM + 1, :])
            shift_ref[head, level : level + 1, :] = shift
            parts.append(split(chosen[0:HEAD_DIM, :] * shift))
        bucket_ref[head], finer_ref[head], outer = through(q_ref[head], parts, cols_ref, head, (0, 1, 2))
        mixed_ref[head] = inner_ref[head] + outer
        gate = gate_ref[head].astype(F32)
        act = gate * jax.nn.sigmoid(gate)
        act_ref[head] = act
        pulled_ref[head] = grad_ref[head].astype(F32) * gain_ref[head : head + 1, :] * act
        wide_q = q_ref[head].astype(F32)
        for level in (3, 4):
            scaled = cols_ref[:, 4 * level + head : 4 * level + head + 1] * wide_q
            high, low = split(scaled)
            at = 3 * HEAD_DIM * (level - 3)
            for i, part in enumerate((high, low, high)):
                scaled_ref[head, :, at + HEAD_DIM * i : at + HEAD_DIM * (i + 1)] = part
            high, low = split(jnp.transpose(scaled))
            turned_ref[head, level - 3, :, 0:WIDTH] = high
            turned_ref[head, level - 3, :, WIDTH:] = low


def mixed_kernel(
    scaled_ref, near_ref, act_ref, pulled_ref, own_ref, other_ref, shifts_ref,
    mixed_ref, pay_ref, bucket_ref, finer_ref, shift_ref,
):
    core = place()[2]
    ones = jnp.ones((8, HEAD_DIM), BF16)
    squares = jnp.zeros((8, WIDTH), F32)
    crosses = jnp.zeros((8, WIDTH), F32)
    for head in range(LOCAL):
        earlier = shifts_ref[head, 7:8, :]
        shift_ref[head] = shifts_ref[head]
        parts = []
        for level in (3, 4):
            chosen = chosen_bucket(own_ref, other_ref, level - 3, head, core)
            shift = jnp.exp(earlier + chosen[HEAD_DIM : HEAD_DIM + 1, :])
            shift_ref[head, level : level + 1, :] = shift
            parts.append(split(chosen[0:HEAD_DIM, :] * shift))
        for i, (high, low) in enumerate(parts):
            piece = slice(HEAD_DIM * i, HEAD_DIM * (i + 1))
            bucket_ref[head, :, piece] = high
            finer_ref[head, :, piece] = low
        stacked = jnp.concatenate([part for high, low in parts for part in (high, high, low)], axis=0)
        mixed = near_ref[head] + dot(scaled_ref[head], stacked, NN)
        mixed_ref[head] = mixed
        gated = mixed * act_ref[head]
        squares = squares + dot(ones, (gated * gated).astype(BF16), NT)
        crosses = crosses + dot(ones, (mixed * pulled_ref[head]).astype(BF16), NT)
    for half in range(2):
        piece = slice(HEAD_DIM * half, HEAD_DIM * (half + 1))
        pay_ref[half : half + 1, :] = squares[0:1, piece]
        pay_ref[2 + half : 3 + half, :] = crosses[0:1, piece]


def add_kernel(a_ref, b_ref, out_ref):
    out_ref[...] = a_ref[...] + b_ref[...]


def gate_kernel(
    turned_ref, mixed_ref, act_ref, pulled_ref, grad_ref, shift_ref, sums_ref, three_ref, two_ref, one_ref,
    g_ref, scale_ref, keep_ref, send_ref,
):
    x, _, core = place()
    ones = jnp.ones((8, HEAD_DIM), F32)
    sums = (sums_ref[...] + three_ref[...]) + (two_ref[...] + one_ref[...])
    sums = jnp.concatenate([sums, jnp.zeros_like(sums)], axis=0)
    row = iotas((8, HEAD_DIM))[0]
    wide = [dot(jnp.where(row == i, sums, 0.0), ones, TN, HIGH) for i in range(4)]
    squares = jnp.concatenate(wide[0:2], axis=0)
    crosses = jnp.concatenate(wide[2:4], axis=0)
    inverse = lax.rsqrt(squares * (1.0 / TOTAL) + EPSILON)
    pull = inverse * inverse * inverse * crosses * (1.0 / TOTAL)
    scale_ref[0] = inverse
    scale_ref[1] = pull
    gains = []
    for ref in (keep_ref, send_ref):
        ref[:, :, HEAD_DIM:, :] = jnp.zeros((2, 2, 8, HEAD_DIM), F32)
    for head in range(LOCAL):
        act = act_ref[head]
        gated = mixed_ref[head] * act
        gains.append(jnp.sum(grad_ref[head].astype(F32) * (gated * inverse), axis=0, keepdims=True))
        g = (inverse * pulled_ref[head] - gated * act * pull).astype(BF16)
        g_ref[head] = g
        twice = jnp.concatenate([g, g], axis=0)
        far = [dot(turned_ref[head, i], twice, NN) * shift_ref[head, 3 + i : 4 + i, :] for i in range(2)]
        near = jnp.where(lax.rem(x, 2) == 1, far[0], far[1])

        def put(ref):
            ref[0, head % 2, 0:HEAD_DIM, :] = near
            ref[1, head % 2, 0:HEAD_DIM, :] = far[1]

        pl.when(core == head // 2)(lambda: put(keep_ref))
        pl.when(core != head // 2)(lambda: put(send_ref))
    for head in range(LOCAL):
        for ref in (keep_ref, send_ref):
            ref[0, 0, HEAD_DIM + head : HEAD_DIM + head + 1, :] = gains[head]
            ref[1, 0, HEAD_DIM + head : HEAD_DIM + head + 1, :] = gains[head]


def reached(q, g, cols_ref, shift_ref, head, levels):
    parts = [split(cols_ref[:, 4 * level + head : 4 * level + head + 1] * g) for level in levels]
    both = dot(q, jnp.concatenate([part for pair in parts for part in pair], axis=1), TN)
    found = []
    for i, level in enumerate(levels):
        at = 2 * HEAD_DIM * i
        grad = both[:, at : at + HEAD_DIM] + both[:, at + HEAD_DIM : at + 2 * HEAD_DIM]
        found.append(grad * shift_ref[head, level : level + 1, :])
    return found


def meet_kernel(keep_ref, other_ref, near_ref, far_ref):
    near_ref[...] = keep_ref[0] + other_ref[0]
    far_ref[...] = keep_ref[1] + other_ref[1]


def close_kernel(
    q_ref, g_ref, mixed_ref, gate_ref, grad_ref, gain_ref, cols_ref, shift_ref, scale_ref,
    out_ref, grad_gate_ref, keep_ref, send_ref, zeroth_ref,
):
    core = place()[2]
    inverse, pull = scale_ref[0], scale_ref[1]
    for ref in (keep_ref, send_ref):
        ref[:, :, HEAD_DIM:, :] = jnp.zeros((2, 2, 8, HEAD_DIM), F32)
    for head in range(LOCAL):
        near = reached(q_ref[head], g_ref[head].astype(F32), cols_ref, shift_ref, head, (0, 1, 2))
        zeroth_ref[head] = near[0]

        def put(ref):
            ref[0, head % 2, 0:HEAD_DIM, :] = near[1]
            ref[1, head % 2, 0:HEAD_DIM, :] = near[2]

        pl.when(core == head // 2)(lambda: put(keep_ref))
        pl.when(core != head // 2)(lambda: put(send_ref))
    for head in range(LOCAL):
        gain = gain_ref[head : head + 1, :]
        gate = gate_ref[head].astype(F32)
        sigmoid = jax.nn.sigmoid(gate)
        mixed = mixed_ref[head]
        gated = mixed * (gate * sigmoid)
        out_ref[head] = (gain * (gated * inverse)).astype(BF16)
        grad_gated = inverse * (grad_ref[head].astype(F32) * gain) - gated * pull
        grad_gate_ref[head] = (grad_gated * mixed * sigmoid * (1.0 + gate * (1.0 - sigmoid))).astype(BF16)


def down_kernel(
    own_ref, one_ref, two_ref, three_ref, near_ref, near_other_ref, info_ref, wide_ref,
    m0_ref, m1_ref, m2_ref, m3_ref,
):
    x, y, _ = place()
    refs = (own_ref, one_ref, two_ref, three_ref)
    carry_x = jnp.exp(wide_ref[:, 1:2, :])
    first = x == 0
    c1 = flag(x <= 2)
    c2 = flag(first) * carry_x + flag(x == 1)
    c3 = flag(first) * carry_x
    body = slice(0, HEAD_DIM)
    state = c1 * one_ref[:, body, :] + c2 * two_ref[:, body, :] + c3 * three_ref[:, body, :]
    tails = [ref[:, HEAD_DIM:, :] for ref in refs]
    where = [lax.rem(x + step, 4) for step in range(4)]
    by_x = [sum(flag(where[i] == j) * tails[i] for i in range(4)) for j in range(4)]
    gains = ((by_x[0] + by_x[1]) + by_x[2]) + by_x[3]
    low = near_ref[0, :, body, :] + near_other_ref[0, :, body, :]
    high = near_ref[1, :, body, :] + near_other_ref[1, :, body, :]
    totals = [info_ref[:, j : j + 1, :] for j in range(4)]
    after = [totals[1] + totals[2] + totals[3], totals[2] + totals[3], totals[3], jnp.zeros_like(totals[3])]
    after = [jnp.exp(part) for part in after]
    carry_y = jnp.exp(totals[1])
    for step, ref in enumerate((m0_ref, m1_ref, m2_ref, m3_ref)):
        to = order(y, step)
        message = sum(flag(to == j) * after[j] for j in range(4)) * state
        if step == 1:
            message = message + flag(lax.rem(y, 2) == 1) * low
        if step:
            message = message + flag(y >= 2) * (flag(to == 1) + flag(to == 0) * carry_y) * high
        ref[:, body, :] = message
        ref[:, HEAD_DIM:, :] = gains


def backward_kernel(
    q_ref, k_ref, v_ref, g_ref, mix_ref, weight_ref, scored_ref, bucket_ref, finer_ref, far_ref, far_finer_ref, cols_ref, run_ref,
    grad_q_ref, grad_k_ref, grad_v_ref, levels_ref,
):
    early, late = iotas((WIDTH, WIDTH))
    crossed = jnp.bitwise_xor(early, late)
    ones = jnp.ones((8, HEAD_DIM), BF16)
    for level in range(DEPTH + 1 + INTER, LEVELS):
        levels_ref[level] = jnp.zeros((LOCAL, WIDTH), F32)
    for head in range(LOCAL):
        q, k, v, g = q_ref[head], k_ref[head], v_ref[head], g_ref[head]
        grad_mixing = dot(v, g, NT)
        grad_scores = (grad_mixing * weight_ref[head]).astype(BF16)
        grad_k_ref[head] = dot(grad_scores, q, NN)
        grad_v_ref[head] = dot(mix_ref[head], g, NN)
        grad_q = dot(grad_scores, k, TN)
        moved = grad_mixing * scored_ref[head]
        for level in range(DEPTH + 1):
            inside = crossed == 0
            if level:
                inside = (crossed >= 2 ** (level - 1)) & (crossed < 2**level)
            levels_ref[level, head : head + 1, :] = jnp.sum(jnp.where(inside, moved, 0.0), axis=0, keepdims=True)
        wide_q = q.astype(F32)
        grown = jnp.exp(run_ref[head : head + 1, :])
        for level in range(INTER):
            high, low = (bucket_ref, finer_ref) if level < 3 else (far_ref, far_finer_ref)
            piece = slice(HEAD_DIM * (level % 3), HEAD_DIM * (level % 3 + 1))
            pulled = dot(g, high[head, :, piece], NT) + dot(g, low[head, :, piece], NT)
            at = 4 * level + head
            grad_q = grad_q + cols_ref[:, at : at + 1] * pulled
            high, low = split(wide_q * pulled)
            sums = dot(ones, high, NT) + dot(ones, low, NT)
            levels_ref[DEPTH + 1 + level, head : head + 1, :] = grown * sums[0:1, :]
        grad_q_ref[head] = grad_q.astype(BF16)


def join_kernel(own_ref, one_ref, two_ref, three_ref, half_ref, sum_ref):
    y = place()[1]
    refs = (own_ref, one_ref, two_ref, three_ref)
    where = [lax.rem(y + step, 4) for step in range(4)]
    tails = [ref[0, HEAD_DIM : HEAD_DIM + LOCAL, :] for ref in refs]
    by_y = [sum(flag(where[i] == j) * tails[i] for i in range(4)) for j in range(4)]
    sum_ref[...] = ((by_y[0] + by_y[1]) + by_y[2]) + by_y[3]
    half_ref[...] = sum(ref[:, 0:HEAD_DIM, :] for ref in refs)


def final_kernel(
    k_ref, v_ref, cols_ref, half_ref, other_ref, zeroth_ref, first_ref, grad_k_ref, grad_v_ref, sum_ref,
    out_k_ref, out_v_ref, gain_ref,
):
    gain_ref[...] = sum_ref[...]
    core = place()[2]
    even = core == 0
    for head in range(LOCAL):
        slot = head % 2
        half = jnp.where(core == head // 2, half_ref[slot], other_ref[slot])
        carry = jnp.exp(first_ref[0, HEAD_DIM + 4 + head : HEAD_DIM + 5 + head, :])
        high, low = split(jnp.where(even, carry * half + zeroth_ref[head], half))
        tail = cols_ref[:, 24 + head : 25 + head]
        k, v = k_ref[head], v_ref[head]
        out_k_ref[head] = (grad_k_ref[head] + tail * (dot(v, high, NT) + dot(v, low, NT))).astype(BF16)
        out_v_ref[head] = (grad_v_ref[head] + tail * (dot(k, high, NN) + dot(k, low, NN))).astype(BF16)


def call(kernel, outs, *args, scratch=(), flops=0, hbm=(), limit=12):
    size = sum(a.size * a.dtype.itemsize for a in args)
    shapes = [jax.ShapeDtypeStruct(shape, kind) for shape, kind in outs]
    size += sum(s.size * s.dtype.itemsize for s in shapes)
    spaces = [pltpu.HBM if i in hbm else pltpu.VMEM for i in range(len(args))]
    return pl.pallas_call(
        kernel,
        out_shape=shapes,
        in_specs=[pl.BlockSpec(memory_space=space) for space in spaces],
        scratch_shapes=list(scratch),
        cost_estimate=pl.CostEstimate(flops=flops, bytes_accessed=size, transcendentals=0),
        compiler_params=pltpu.CompilerParams(vmem_limit_bytes=limit * 2**20),
    )(*args)


def layer(queries, keys, values, log_decay, level_weight, gate_input, norm_gain, out_grad):
    level_rows = jnp.transpose(level_weight, (1, 0, 2))
    message = ((2, ROWS, HEAD_DIM), F32)
    double = ((2, 2, ROWS, HEAD_DIM), F32)
    tokens = (LOCAL, WIDTH, HEAD_DIM)
    square = (LOCAL, WIDTH, WIDTH)
    info = ((2, 8, HEAD_DIM), F32)
    columns = ((WIDTH, HEAD_DIM), F32)

    keep, away, running = call(
        state_kernel,
        [message, message, ((LOCAL, WIDTH), F32)],
        *(pltpu.with_memory_space_constraint(a, pltpu.HBM) for a in (log_decay, keys, values)),
        scratch=[
            pltpu.VMEM((LOCAL, WIDTH), F32), pltpu.VMEM(tokens, BF16), pltpu.VMEM(tokens, BF16),
            pltpu.VMEM((16, WIDTH), F32), pltpu.SemaphoreType.DMA((3,)),
        ],
        hbm=(0, 1, 2),
    )
    first = send(away, SWAP)
    (chip,) = call(pair_kernel, [message], keep, first)
    from_y = [send(chip, along_y(step)) for step in (1, 2, 3)]
    rest = send(keep, UP)
    inner, mixing, weight, scored, cols = call(
        intra_kernel,
        [(tokens, F32), (square, BF16), (square, F32), (square, F32), columns],
        queries, keys, values, level_rows, running,
        scratch=[pltpu.VMEM((HEAD_DIM, WIDTH), F32)],
        flops=10**9,
    )
    row, near, totals_y = call(y_kernel, [message, double, info], chip, *from_y)
    from_x = [send(row, along_x(step)) for step in (1, 2, 3)]
    near_other = send(near, SWAP)
    far, totals_x = call(x_kernel, [double, info], row, *from_x, totals_y)
    far_other = send(far, SWAP)
    near_kind = ((LOCAL, HEAD_DIM, 3 * HEAD_DIM), BF16)
    far_kind = ((LOCAL, HEAD_DIM, 2 * HEAD_DIM), BF16)
    rows = ((LOCAL, 8, HEAD_DIM), F32)
    scaled_kind = ((LOCAL, WIDTH, 6 * HEAD_DIM), BF16)
    turned_kind = ((LOCAL, 2, HEAD_DIM, 2 * WIDTH), BF16)
    near_mixed, act, pulled, bucket, finer, shifts, scaled_q, turned_q = call(
        near_kernel,
        [(tokens, F32)] * 3 + [near_kind, near_kind, rows, scaled_kind, turned_kind],
        queries, inner, gate_input, out_grad, norm_gain, cols, near, near_other, first, rest,
        flops=10**9,
    )
    mixed, pay, far_bucket, far_finer, shift = call(
        mixed_kernel,
        [(tokens, F32), ((4, HEAD_DIM), F32), far_kind, far_kind, rows],
        scaled_q, near_mixed, act, pulled, far, far_other, shifts,
    )
    (pay,) = call(add_kernel, [((4, HEAD_DIM), F32)], pay, along_z(pay, both_ways(Z_PAIRS)))
    others = [along_z(pay, pairs) for pairs in (both_ways(Z_FAR), Z_TWO, both_ways(Z_NEXT))]
    grad_mixed, scale, far_keep, far_away = call(
        gate_kernel,
        [(tokens, BF16), ((2, WIDTH, HEAD_DIM), F32), double, double],
        turned_q, mixed, act, pulled, out_grad, shift, pay, *others,
    )
    to_one, to_far = call(meet_kernel, [message] * 2, far_keep, send(far_away, SWAP))
    back_x = [send(to_one, along_x(-1)), send(to_far, along_x(-2)), send(to_far, along_x(-3))]
    layer_out, grad_gate, near_keep, near_away, zeroth = call(
        close_kernel,
        [(tokens, BF16)] * 2 + [double] * 2 + [((LOCAL, HEAD_DIM, HEAD_DIM), F32)],
        queries, grad_mixed, mixed, gate_input, out_grad, norm_gain, cols, shift, scale,
        flops=10**9,
    )
    near_back = send(near_away, SWAP)
    messages = call(down_kernel, [message] * 4, to_far, *back_x, near_keep, near_back, totals_y, totals_x)
    back_y = [messages[0]] + [send(messages[step], along_y(-step)) for step in (1, 2, 3)]
    zeroth_back = send(zeroth, DOWN)
    grad_queries, grad_k, grad_v, levels = call(
        backward_kernel,
        [(tokens, BF16), (tokens, F32), (tokens, F32), ((LEVELS, LOCAL, WIDTH), F32)],
        queries, keys, values, grad_mixed, mixing, weight, scored, bucket, finer, far_bucket, far_finer, cols, running,
        flops=10**9,
    )
    half, gain_sum = call(join_kernel, [((2, HEAD_DIM, HEAD_DIM), F32), ((LOCAL, HEAD_DIM), F32)], *back_y)
    half_other = send(half, SWAP)
    grad_keys, grad_values, grad_gain = call(
        final_kernel,
        [(tokens, BF16)] * 2 + [((LOCAL, HEAD_DIM), F32)],
        keys, values, cols, half, half_other, zeroth_back, first, grad_k, grad_v, gain_sum,
    )
    grad_levels = jnp.transpose(levels, (1, 0, 2))
    return (layer_out, grad_queries, grad_keys, grad_values, grad_levels, grad_gate, grad_gain)


def solution(mesh):
    rows = P("head", "seq", None)
    in_specs = (rows, rows, rows, P("head", "seq"), P("head", None, "seq"), rows, P("head", None), rows)
    out_specs = (rows, rows, rows, rows, P("head", None, "seq"), rows, P("head", None))
    return jax.shard_map(layer, mesh=mesh, in_specs=in_specs, out_specs=out_specs, check_vma=False)
```

```python
import jax
import jax.numpy as jnp
from jax import lax
from jax.experimental import pallas as pl
from jax.experimental.pallas import tpu as pltpu
from jax.sharding import PartitionSpec as P


HEADS = 32
HEAD_DIM = 128
TOTAL = HEADS * HEAD_DIM
EPSILON = 1e-05
F32 = jnp.float32
BF16 = jnp.bfloat16

LOCAL = 4
WIDTH = 256
DEPTH = 8
INTER = 5
LEVELS = 21
ROWS = HEAD_DIM + 8


def place():
    me = lax.axis_index("seq")
    return me // 8, lax.rem(me // 2, 4), lax.rem(me, 2)


def ring(function):
    pairs = []
    for x in range(4):
        for y in range(4):
            for core in range(2):
                to = function(x, y, core)
                if to is not None:
                    pairs.append(((x * 4 + y) * 2 + core, (to[0] * 4 + to[1]) * 2 + to[2]))
    return pairs


SWAP = ring(lambda x, y, core: (x, y, 1 - core))
UP = ring(lambda x, y, core: (x, y, 1) if core == 0 else None)
DOWN = ring(lambda x, y, core: (x, y, 0) if core == 1 else None)


Z_PAIRS = ((0, 1), (2, 3), (4, 5), (6, 7))
Z_FAR = ((1, 4), (3, 6), (5, 0), (7, 2))
Z_NEXT = ((1, 2), (3, 4), (5, 6), (7, 0))
Z_TWO = [(z, (z + 6 + 4 * (z % 2)) % 8) for z in range(8)]


def both_ways(pairs):
    return [pair for a, b in pairs for pair in ((a, b), (b, a))]


def along_z(array, pairs):
    return lax.ppermute(array, "head", pairs)


def along_y(step):
    return ring(lambda x, y, core: (x, (y + step) % 4, core))


def along_x(step):
    return ring(lambda x, y, core: ((x + step) % 4, y, core))


def send(array, pairs):
    return lax.ppermute(array, "seq", pairs)


def split(array):
    high = array.astype(BF16)
    return high, (array - high.astype(F32)).astype(BF16)


def flag(condition):
    return condition.astype(F32)


def dot(a, b, dims, precision=None):
    return lax.dot_general(a, b, (dims, ((), ())), precision=precision, preferred_element_type=F32)


NN = ((1,), (0,))
NT = ((1,), (1,))
TN = ((0,), (0,))


def iotas(shape):
    return lax.broadcasted_iota(jnp.int32, shape, 0), lax.broadcasted_iota(jnp.int32, shape, 1)


def state_kernel(
    decay_hbm, k_hbm, v_hbm, keep_ref, send_ref, run_ref, decay_ref, k_ref, v_ref, rows_ref, sems
):
    copies = [
        pltpu.make_async_copy(source, to, sems.at[i])
        for i, (source, to) in enumerate(((decay_hbm, decay_ref), (v_hbm, v_ref), (k_hbm, k_ref)))
    ]
    for copy in copies:
        copy.start()
    core = place()[2]
    early, late = iotas((WIDTH, WIDTH))
    upper = (early <= late).astype(F32).astype(BF16)
    copies[0].wait()
    decay = decay_ref[...]
    first = decay.astype(BF16).astype(F32)
    second = (decay - first).astype(BF16).astype(F32)
    rows_ref[0:4, :] = first
    rows_ref[4:8, :] = second
    rows_ref[8:12, :] = decay - first - second
    rows_ref[12:16, :] = jnp.zeros((4, WIDTH), F32)
    parts = dot(rows_ref[...].astype(BF16), upper, NN)
    running = parts[0:4, :] + parts[4:8, :] + parts[8:12, :]
    run_ref[...] = running
    rows_ref[0:4, :] = jnp.exp(running[:, WIDTH - 1 :] - running)
    tails = jnp.transpose(rows_ref[...])
    for copy in copies[1:]:
        copy.wait()
    for head in range(LOCAL):
        weighted = v_ref[head].astype(F32) * tails[:, head : head + 1]
        both = dot(k_ref[head], jnp.concatenate(split(weighted), axis=1), TN)
        state = both[:, 0:HEAD_DIM] + both[:, HEAD_DIM:]
        total = jnp.broadcast_to(running[head : head + 1, WIDTH - 1 :], (4, HEAD_DIM))
        totals = jnp.broadcast_to(running[:, WIDTH - 1 :], (4, HEAD_DIM))

        def put(ref):
            ref[head % 2, 0:HEAD_DIM, :] = state
            ref[head % 2, HEAD_DIM : HEAD_DIM + 4, :] = total
            ref[head % 2, HEAD_DIM + 4 :, :] = totals

        pl.when(core == head // 2)(lambda: put(keep_ref))
        pl.when(core != head // 2)(lambda: put(send_ref))


def pair_kernel(keep_ref, first_ref, chip_ref):
    late = place()[2] == 1
    before = jnp.where(late, first_ref[...], keep_ref[...])
    after = jnp.where(late, keep_ref[...], first_ref[...])
    carry = jnp.exp(after[:, HEAD_DIM : HEAD_DIM + 1, :])
    chip_ref[:, 0:HEAD_DIM, :] = carry * before[:, 0:HEAD_DIM, :] + after[:, 0:HEAD_DIM, :]
    chip_ref[:, HEAD_DIM:, :] = before[:, HEAD_DIM:, :] + after[:, HEAD_DIM:, :]


def intra_kernel(
    q_ref, k_ref, v_ref, level_ref, run_ref, inner_ref, mix_ref, weight_ref, scored_ref, cols_ref, rows_ref
):
    running = run_ref[...]
    grown = jnp.exp(running)
    rows_ref[...] = jnp.zeros_like(rows_ref)
    for level in range(INTER):
        rows_ref[4 * level : 4 * level + 4, :] = level_ref[DEPTH + 1 + level] * grown
    rows_ref[20:24, :] = running
    rows_ref[24:28, :] = jnp.exp(running[:, WIDTH - 1 :] - running)
    cols_ref[...] = jnp.transpose(rows_ref[...])
    early, late = iotas((WIDTH, WIDTH))
    crossed = jnp.bitwise_xor(early, late)
    causal = early <= late
    for head in range(LOCAL):
        spread = run_ref[head : head + 1, :] - cols_ref[:, 20 + head : 21 + head]
        decay = jnp.where(causal, jnp.exp(jnp.where(causal, spread, 0.0)), 0.0)
        chosen = jnp.broadcast_to(level_ref[0, head : head + 1, :], (WIDTH, WIDTH))
        for level in range(1, DEPTH + 1):
            chosen = jnp.where(crossed >= 2 ** (level - 1), level_ref[level, head : head + 1, :], chosen)
        scored = dot(k_ref[head], q_ref[head], NT)
        weight = decay * chosen
        mixing = (scored * weight).astype(BF16)
        weight_ref[head] = weight
        scored_ref[head] = scored * decay
        mix_ref[head] = mixing
        inner_ref[head] = dot(mixing, v_ref[head], TN)


def order(position, step):
    return lax.rem(position + 4 - step, 4)


def y_kernel(own_ref, one_ref, two_ref, three_ref, next_ref, bucket_ref, info_ref):
    y = place()[1]
    refs = (own_ref, one_ref, two_ref, three_ref)
    where = [order(y, step) for step in range(4)]
    totals = [ref[:, HEAD_DIM : HEAD_DIM + 1, :] for ref in refs]
    by_y = [sum(flag(where[i] == j) * totals[i] for i in range(4)) for j in range(4)]
    carry = jnp.exp(by_y[1])
    whole = jnp.zeros((2, HEAD_DIM, HEAD_DIM), F32)
    pair = jnp.zeros((2, HEAD_DIM, HEAD_DIM), F32)
    for i in range(4):
        state = refs[i][:, 0:HEAD_DIM, :]
        later = sum(flag(j > where[i]) * by_y[j] for j in range(1, 4))
        whole = whole + jnp.exp(later) * state
        if i:
            part = flag(y >= 2) * (flag(where[i] == 1) + flag(where[i] == 0) * carry)
            pair = pair + part * state
    below = sum(flag(j < y) * by_y[j] for j in range(3))
    next_ref[:, 0:HEAD_DIM, :] = whole
    next_ref[:, HEAD_DIM:, :] = jnp.broadcast_to(by_y[0] + by_y[1] + by_y[2] + by_y[3], (2, 8, HEAD_DIM))
    bucket_ref[0, :, 0:HEAD_DIM, :] = flag(lax.rem(y, 2) == 1) * one_ref[:, 0:HEAD_DIM, :]
    bucket_ref[0, :, HEAD_DIM:, :] = jnp.zeros((2, 8, HEAD_DIM), F32)
    bucket_ref[1, :, 0:HEAD_DIM, :] = pair
    bucket_ref[1, :, HEAD_DIM:, :] = jnp.broadcast_to(flag(y == 3) * by_y[2], (2, 8, HEAD_DIM))
    for j in range(4):
        info_ref[:, j : j + 1, :] = by_y[j]
    info_ref[:, 4:8, :] = jnp.broadcast_to(below, (2, 4, HEAD_DIM))


def x_kernel(own_ref, one_ref, two_ref, three_ref, info_ref, bucket_ref, wide_ref):
    x = place()[0]
    refs = (own_ref, one_ref, two_ref, three_ref)
    where = [order(x, step) for step in range(4)]
    totals = [ref[:, HEAD_DIM : HEAD_DIM + 1, :] for ref in refs]
    by_x = [sum(flag(where[i] == j) * totals[i] for i in range(4)) for j in range(4)]
    carry = jnp.exp(by_x[1])
    pair = jnp.zeros((2, HEAD_DIM, HEAD_DIM), F32)
    for i in range(1, 4):
        part = flag(x >= 2) * (flag(where[i] == 1) + flag(where[i] == 0) * carry)
        pair = pair + part * refs[i][:, 0:HEAD_DIM, :]
    below = info_ref[:, 4:5, :]
    bucket_ref[0, :, 0:HEAD_DIM, :] = flag(lax.rem(x, 2) == 1) * one_ref[:, 0:HEAD_DIM, :]
    bucket_ref[0, :, HEAD_DIM:, :] = jnp.broadcast_to(below, (2, 8, HEAD_DIM))
    bucket_ref[1, :, 0:HEAD_DIM, :] = pair
    bucket_ref[1, :, HEAD_DIM:, :] = jnp.broadcast_to(below + flag(x == 3) * by_x[2], (2, 8, HEAD_DIM))
    for j in range(4):
        wide_ref[:, j : j + 1, :] = by_x[j]
        wide_ref[:, 4 + j : 5 + j, :] = by_x[j]


def through(q, parts, cols_ref, head, levels):
    bucket, finer = (jnp.concatenate([part[i] for part in parts], axis=1) for i in range(2))
    found = dot(q, bucket, NN) + dot(q, finer, NN)
    outer = sum(
        cols_ref[:, 4 * level + head : 4 * level + head + 1] * found[:, HEAD_DIM * i : HEAD_DIM * (i + 1)]
        for i, level in enumerate(levels)
    )
    return bucket, finer, outer


def chosen_bucket(own_ref, other_ref, at, head, core):
    return jnp.where(core == head // 2, own_ref[at, head % 2], other_ref[at, head % 2])


def near_kernel(
    q_ref, inner_ref, gate_ref, grad_ref, gain_ref, cols_ref, own_ref, other_ref, first_ref, rest_ref,
    mixed_ref, act_ref, pulled_ref, bucket_ref, finer_ref, shift_ref, scaled_ref, turned_ref,
):
    core = place()[2]
    odd = flag(core == 1)
    for head in range(LOCAL):
        slot = head % 2
        zeroth = rest_ref[slot, 0:HEAD_DIM, :] if head < 2 else first_ref[slot, 0:HEAD_DIM, :]
        earlier = odd * first_ref[0, HEAD_DIM + 4 + head : HEAD_DIM + 5 + head, :]
        parts = [split(odd * zeroth)]
        shift_ref[head] = jnp.ones((8, HEAD_DIM), F32)
        shift_ref[head, 7:8, :] = earlier
        for level in (1, 2):
            chosen = chosen_bucket(own_ref, other_ref, level - 1, head, core)
            shift = jnp.exp(earlier + chosen[HEAD_DIM : HEAD_DIM + 1, :])
            shift_ref[head, level : level + 1, :] = shift
            parts.append(split(chosen[0:HEAD_DIM, :] * shift))
        bucket_ref[head], finer_ref[head], outer = through(q_ref[head], parts, cols_ref, head, (0, 1, 2))
        mixed_ref[head] = inner_ref[head] + outer
        gate = gate_ref[head].astype(F32)
        act = gate * jax.nn.sigmoid(gate)
        act_ref[head] = act
        pulled_ref[head] = grad_ref[head].astype(F32) * gain_ref[head : head + 1, :] * act
        wide_q = q_ref[head].astype(F32)
        for level in (3, 4):
            scaled = cols_ref[:, 4 * level + head : 4 * level + head + 1] * wide_q
            high, low = split(scaled)
            at = 3 * HEAD_DIM * (level - 3)
            for i, part in enumerate((high, low, high)):
                scaled_ref[head, :, at + HEAD_DIM * i : at + HEAD_DIM * (i + 1)] = part
            high, low = split(jnp.transpose(scaled))
            turned_ref[head, level - 3, :, 0:WIDTH] = high
            turned_ref[head, level - 3, :, WIDTH:] = low


def mixed_kernel(
    scaled_ref, near_ref, act_ref, pulled_ref, own_ref, other_ref, shifts_ref,
    mixed_ref, pay_ref, bucket_ref, finer_ref, shift_ref,
):
    core = place()[2]
    ones = jnp.ones((8, HEAD_DIM), BF16)
    squares = jnp.zeros((8, WIDTH), F32)
    crosses = jnp.zeros((8, WIDTH), F32)
    for head in range(LOCAL):
        earlier = shifts_ref[head, 7:8, :]
        shift_ref[head] = shifts_ref[head]
        parts = []
        for level in (3, 4):
            chosen = chosen_bucket(own_ref, other_ref, level - 3, head, core)
            shift = jnp.exp(earlier + chosen[HEAD_DIM : HEAD_DIM + 1, :])
            shift_ref[head, level : level + 1, :] = shift
            parts.append(split(chosen[0:HEAD_DIM, :] * shift))
        for i, (high, low) in enumerate(parts):
            piece = slice(HEAD_DIM * i, HEAD_DIM * (i + 1))
            bucket_ref[head, :, piece] = high
            finer_ref[head, :, piece] = low
        stacked = jnp.concatenate([part for high, low in parts for part in (high, high, low)], axis=0)
        mixed = near_ref[head] + dot(scaled_ref[head], stacked, NN)
        mixed_ref[head] = mixed
        gated = mixed * act_ref[head]
        squares = squares + dot(ones, (gated * gated).astype(BF16), NT)
        crosses = crosses + dot(ones, (mixed * pulled_ref[head]).astype(BF16), NT)
    for half in range(2):
        piece = slice(HEAD_DIM * half, HEAD_DIM * (half + 1))
        pay_ref[half : half + 1, :] = squares[0:1, piece]
        pay_ref[2 + half : 3 + half, :] = crosses[0:1, piece]


def add_kernel(a_ref, b_ref, out_ref):
    out_ref[...] = a_ref[...] + b_ref[...]


def gate_kernel(
    turned_ref, mixed_ref, act_ref, pulled_ref, grad_ref, shift_ref, sums_ref, three_ref, two_ref, one_ref,
    g_ref, scale_ref, keep_ref, send_ref,
):
    x, _, core = place()
    sums = (sums_ref[...] + three_ref[...]) + (two_ref[...] + one_ref[...])
    first = sums.astype(BF16).astype(F32)
    second = (sums - first).astype(BF16).astype(F32)
    parts = jnp.concatenate([first, second, sums - first - second, jnp.zeros_like(sums)], axis=0).astype(BF16)
    row, column = iotas((16, 4 * HEAD_DIM))
    chosen = ((row < 12) & (lax.rem(row, 4) == column // HEAD_DIM)).astype(F32).astype(BF16)
    wide = dot(parts, chosen, TN)
    squares = jnp.concatenate([wide[:, 0:HEAD_DIM], wide[:, HEAD_DIM : 2 * HEAD_DIM]], axis=0)
    crosses = jnp.concatenate([wide[:, 2 * HEAD_DIM : 3 * HEAD_DIM], wide[:, 3 * HEAD_DIM :]], axis=0)
    inverse = lax.rsqrt(squares * (1.0 / TOTAL) + EPSILON)
    pull = inverse * inverse * inverse * crosses * (1.0 / TOTAL)
    scale_ref[0] = inverse
    scale_ref[1] = pull
    gains = []
    for ref in (keep_ref, send_ref):
        ref[:, :, HEAD_DIM:, :] = jnp.zeros((2, 2, 8, HEAD_DIM), F32)
    for head in range(LOCAL):
        act = act_ref[head]
        gated = mixed_ref[head] * act
        gains.append(jnp.sum(grad_ref[head].astype(F32) * (gated * inverse), axis=0, keepdims=True))
        g = (inverse * pulled_ref[head] - gated * act * pull).astype(BF16)
        g_ref[head] = g
        twice = jnp.concatenate([g, g], axis=0)
        far = [dot(turned_ref[head, i], twice, NN) * shift_ref[head, 3 + i : 4 + i, :] for i in range(2)]
        near = jnp.where(lax.rem(x, 2) == 1, far[0], far[1])

        def put(ref):
            ref[0, head % 2, 0:HEAD_DIM, :] = near
            ref[1, head % 2, 0:HEAD_DIM, :] = far[1]

        pl.when(core == head // 2)(lambda: put(keep_ref))
        pl.when(core != head // 2)(lambda: put(send_ref))
    for head in range(LOCAL):
        for ref in (keep_ref, send_ref):
            ref[0, 0, HEAD_DIM + head : HEAD_DIM + head + 1, :] = gains[head]
            ref[1, 0, HEAD_DIM + head : HEAD_DIM + head + 1, :] = gains[head]


def reached(q, g, cols_ref, shift_ref, head, levels):
    parts = [split(cols_ref[:, 4 * level + head : 4 * level + head + 1] * g) for level in levels]
    both = dot(q, jnp.concatenate([part for pair in parts for part in pair], axis=1), TN)
    found = []
    for i, level in enumerate(levels):
        at = 2 * HEAD_DIM * i
        grad = both[:, at : at + HEAD_DIM] + both[:, at + HEAD_DIM : at + 2 * HEAD_DIM]
        found.append(grad * shift_ref[head, level : level + 1, :])
    return found


def meet_kernel(keep_ref, other_ref, near_ref, far_ref):
    near_ref[...] = keep_ref[0] + other_ref[0]
    far_ref[...] = keep_ref[1] + other_ref[1]


def close_kernel(
    q_ref, g_ref, mixed_ref, gate_ref, grad_ref, gain_ref, cols_ref, shift_ref, scale_ref,
    out_ref, grad_gate_ref, keep_ref, send_ref, zeroth_ref,
):
    core = place()[2]
    inverse, pull = scale_ref[0], scale_ref[1]
    for ref in (keep_ref, send_ref):
        ref[:, :, HEAD_DIM:, :] = jnp.zeros((2, 2, 8, HEAD_DIM), F32)
    for head in range(LOCAL):
        near = reached(q_ref[head], g_ref[head].astype(F32), cols_ref, shift_ref, head, (0, 1, 2))
        zeroth_ref[head] = near[0]

        def put(ref):
            ref[0, head % 2, 0:HEAD_DIM, :] = near[1]
            ref[1, head % 2, 0:HEAD_DIM, :] = near[2]

        pl.when(core == head // 2)(lambda: put(keep_ref))
        pl.when(core != head // 2)(lambda: put(send_ref))
    for head in range(LOCAL):
        gain = gain_ref[head : head + 1, :]
        gate = gate_ref[head].astype(F32)
        sigmoid = jax.nn.sigmoid(gate)
        mixed = mixed_ref[head]
        gated = mixed * (gate * sigmoid)
        out_ref[head] = (gain * (gated * inverse)).astype(BF16)
        grad_gated = inverse * (grad_ref[head].astype(F32) * gain) - gated * pull
        grad_gate_ref[head] = (grad_gated * mixed * sigmoid * (1.0 + gate * (1.0 - sigmoid))).astype(BF16)


def down_kernel(
    own_ref, one_ref, two_ref, three_ref, near_ref, near_other_ref, info_ref, wide_ref,
    m0_ref, m1_ref, m2_ref, m3_ref,
):
    x, y, _ = place()
    refs = (own_ref, one_ref, two_ref, three_ref)
    carry_x = jnp.exp(wide_ref[:, 1:2, :])
    first = x == 0
    c1 = flag(x <= 2)
    c2 = flag(first) * carry_x + flag(x == 1)
    c3 = flag(first) * carry_x
    body = slice(0, HEAD_DIM)
    state = c1 * one_ref[:, body, :] + c2 * two_ref[:, body, :] + c3 * three_ref[:, body, :]
    tails = [ref[:, HEAD_DIM:, :] for ref in refs]
    where = [lax.rem(x + step, 4) for step in range(4)]
    by_x = [sum(flag(where[i] == j) * tails[i] for i in range(4)) for j in range(4)]
    gains = ((by_x[0] + by_x[1]) + by_x[2]) + by_x[3]
    low = near_ref[0, :, body, :] + near_other_ref[0, :, body, :]
    high = near_ref[1, :, body, :] + near_other_ref[1, :, body, :]
    totals = [info_ref[:, j : j + 1, :] for j in range(4)]
    after = [totals[1] + totals[2] + totals[3], totals[2] + totals[3], totals[3], jnp.zeros_like(totals[3])]
    after = [jnp.exp(part) for part in after]
    carry_y = jnp.exp(totals[1])
    for step, ref in enumerate((m0_ref, m1_ref, m2_ref, m3_ref)):
        to = order(y, step)
        message = sum(flag(to == j) * after[j] for j in range(4)) * state
        if step == 1:
            message = message + flag(lax.rem(y, 2) == 1) * low
        if step:
            message = message + flag(y >= 2) * (flag(to == 1) + flag(to == 0) * carry_y) * high
        ref[:, body, :] = message
        ref[:, HEAD_DIM:, :] = gains


def backward_kernel(
    q_ref, k_ref, v_ref, g_ref, mix_ref, weight_ref, scored_ref, bucket_ref, finer_ref, far_ref, far_finer_ref, cols_ref, run_ref,
    grad_q_ref, grad_k_ref, grad_v_ref, levels_ref,
):
    early, late = iotas((WIDTH, WIDTH))
    crossed = jnp.bitwise_xor(early, late)
    ones = jnp.ones((8, HEAD_DIM), BF16)
    for level in range(DEPTH + 1 + INTER, LEVELS):
        levels_ref[level] = jnp.zeros((LOCAL, WIDTH), F32)
    for head in range(LOCAL):
        q, k, v, g = q_ref[head], k_ref[head], v_ref[head], g_ref[head]
        grad_mixing = dot(v, g, NT)
        grad_scores = (grad_mixing * weight_ref[head]).astype(BF16)
        grad_k_ref[head] = dot(grad_scores, q, NN)
        grad_v_ref[head] = dot(mix_ref[head], g, NN)
        grad_q = dot(grad_scores, k, TN)
        moved = grad_mixing * scored_ref[head]
        for level in range(DEPTH + 1):
            inside = crossed == 0
            if level:
                inside = (crossed >= 2 ** (level - 1)) & (crossed < 2**level)
            levels_ref[level, head : head + 1, :] = jnp.sum(jnp.where(inside, moved, 0.0), axis=0, keepdims=True)
        wide_q = q.astype(F32)
        grown = jnp.exp(run_ref[head : head + 1, :])
        for level in range(INTER):
            high, low = (bucket_ref, finer_ref) if level < 3 else (far_ref, far_finer_ref)
            piece = slice(HEAD_DIM * (level % 3), HEAD_DIM * (level % 3 + 1))
            pulled = dot(g, high[head, :, piece], NT) + dot(g, low[head, :, piece], NT)
            at = 4 * level + head
            grad_q = grad_q + cols_ref[:, at : at + 1] * pulled
            high, low = split(wide_q * pulled)
            sums = dot(ones, high, NT) + dot(ones, low, NT)
            levels_ref[DEPTH + 1 + level, head : head + 1, :] = grown * sums[0:1, :]
        grad_q_ref[head] = grad_q.astype(BF16)


def join_kernel(own_ref, one_ref, two_ref, three_ref, half_ref, sum_ref):
    y = place()[1]
    refs = (own_ref, one_ref, two_ref, three_ref)
    where = [lax.rem(y + step, 4) for step in range(4)]
    tails = [ref[0, HEAD_DIM : HEAD_DIM + LOCAL, :] for ref in refs]
    by_y = [sum(flag(where[i] == j) * tails[i] for i in range(4)) for j in range(4)]
    sum_ref[...] = ((by_y[0] + by_y[1]) + by_y[2]) + by_y[3]
    half_ref[...] = sum(ref[:, 0:HEAD_DIM, :] for ref in refs)


def final_kernel(
    k_ref, v_ref, cols_ref, half_ref, other_ref, zeroth_ref, first_ref, grad_k_ref, grad_v_ref, sum_ref,
    out_k_ref, out_v_ref, gain_ref,
):
    gain_ref[...] = sum_ref[...]
    core = place()[2]
    even = core == 0
    for head in range(LOCAL):
        slot = head % 2
        half = jnp.where(core == head // 2, half_ref[slot], other_ref[slot])
        carry = jnp.exp(first_ref[0, HEAD_DIM + 4 + head : HEAD_DIM + 5 + head, :])
        state = jnp.where(even, carry * half + zeroth_ref[head], half).astype(BF16)
        tail = cols_ref[:, 24 + head : 25 + head]
        k, v = k_ref[head], v_ref[head]
        out_k_ref[head] = (grad_k_ref[head] + tail * dot(v, state, NT)).astype(BF16)
        out_v_ref[head] = (grad_v_ref[head] + tail * dot(k, state, NN)).astype(BF16)


def call(kernel, outs, *args, scratch=(), flops=0, hbm=(), limit=12):
    size = sum(a.size * a.dtype.itemsize for a in args)
    shapes = [jax.ShapeDtypeStruct(shape, kind) for shape, kind in outs]
    size += sum(s.size * s.dtype.itemsize for s in shapes)
    spaces = [pltpu.HBM if i in hbm else pltpu.VMEM for i in range(len(args))]
    return pl.pallas_call(
        kernel,
        out_shape=shapes,
        in_specs=[pl.BlockSpec(memory_space=space) for space in spaces],
        scratch_shapes=list(scratch),
        cost_estimate=pl.CostEstimate(flops=flops, bytes_accessed=size, transcendentals=0),
        compiler_params=pltpu.CompilerParams(vmem_limit_bytes=limit * 2**20),
    )(*args)


def layer(queries, keys, values, log_decay, level_weight, gate_input, norm_gain, out_grad):
    level_rows = jnp.transpose(level_weight, (1, 0, 2))
    message = ((2, ROWS, HEAD_DIM), F32)
    double = ((2, 2, ROWS, HEAD_DIM), F32)
    tokens = (LOCAL, WIDTH, HEAD_DIM)
    square = (LOCAL, WIDTH, WIDTH)
    info = ((2, 8, HEAD_DIM), F32)
    columns = ((WIDTH, HEAD_DIM), F32)

    keep, away, running = call(
        state_kernel,
        [message, message, ((LOCAL, WIDTH), F32)],
        *(pltpu.with_memory_space_constraint(a, pltpu.HBM) for a in (log_decay, keys, values)),
        scratch=[
            pltpu.VMEM((LOCAL, WIDTH), F32), pltpu.VMEM(tokens, BF16), pltpu.VMEM(tokens, BF16),
            pltpu.VMEM((16, WIDTH), F32), pltpu.SemaphoreType.DMA((3,)),
        ],
        hbm=(0, 1, 2),
    )
    first = send(away, SWAP)
    (chip,) = call(pair_kernel, [message], keep, first)
    from_y = [send(chip, along_y(step)) for step in (1, 2, 3)]
    rest = send(keep, UP)
    inner, mixing, weight, scored, cols = call(
        intra_kernel,
        [(tokens, F32), (square, BF16), (square, F32), (square, F32), columns],
        queries, keys, values, level_rows, running,
        scratch=[pltpu.VMEM((HEAD_DIM, WIDTH), F32)],
        flops=10**9,
    )
    row, near, totals_y = call(y_kernel, [message, double, info], chip, *from_y)
    from_x = [send(row, along_x(step)) for step in (1, 2, 3)]
    near_other = send(near, SWAP)
    far, totals_x = call(x_kernel, [double, info], row, *from_x, totals_y)
    far_other = send(far, SWAP)
    near_kind = ((LOCAL, HEAD_DIM, 3 * HEAD_DIM), BF16)
    far_kind = ((LOCAL, HEAD_DIM, 2 * HEAD_DIM), BF16)
    rows = ((LOCAL, 8, HEAD_DIM), F32)
    scaled_kind = ((LOCAL, WIDTH, 6 * HEAD_DIM), BF16)
    turned_kind = ((LOCAL, 2, HEAD_DIM, 2 * WIDTH), BF16)
    near_mixed, act, pulled, bucket, finer, shifts, scaled_q, turned_q = call(
        near_kernel,
        [(tokens, F32)] * 3 + [near_kind, near_kind, rows, scaled_kind, turned_kind],
        queries, inner, gate_input, out_grad, norm_gain, cols, near, near_other, first, rest,
        flops=10**9,
    )
    mixed, pay, far_bucket, far_finer, shift = call(
        mixed_kernel,
        [(tokens, F32), ((4, HEAD_DIM), F32), far_kind, far_kind, rows],
        scaled_q, near_mixed, act, pulled, far, far_other, shifts,
    )
    (pay,) = call(add_kernel, [((4, HEAD_DIM), F32)], pay, along_z(pay, both_ways(Z_PAIRS)))
    others = [along_z(pay, pairs) for pairs in (both_ways(Z_FAR), Z_TWO, both_ways(Z_NEXT))]
    grad_mixed, scale, far_keep, far_away = call(
        gate_kernel,
        [(tokens, BF16), ((2, WIDTH, HEAD_DIM), F32), double, double],
        turned_q, mixed, act, pulled, out_grad, shift, pay, *others,
    )
    to_one, to_far = call(meet_kernel, [message] * 2, far_keep, send(far_away, SWAP))
    back_x = [send(to_one, along_x(-1)), send(to_far, along_x(-2)), send(to_far, along_x(-3))]
    layer_out, grad_gate, near_keep, near_away, zeroth = call(
        close_kernel,
        [(tokens, BF16)] * 2 + [double] * 2 + [((LOCAL, HEAD_DIM, HEAD_DIM), F32)],
        queries, grad_mixed, mixed, gate_input, out_grad, norm_gain, cols, shift, scale,
        flops=10**9,
    )
    near_back = send(near_away, SWAP)
    messages = call(down_kernel, [message] * 4, to_far, *back_x, near_keep, near_back, totals_y, totals_x)
    back_y = [messages[0]] + [send(messages[step], along_y(-step)) for step in (1, 2, 3)]
    zeroth_back = send(zeroth, DOWN)
    grad_queries, grad_k, grad_v, levels = call(
        backward_kernel,
        [(tokens, BF16), (tokens, F32), (tokens, F32), ((LEVELS, LOCAL, WIDTH), F32)],
        queries, keys, values, grad_mixed, mixing, weight, scored, bucket, finer, far_bucket, far_finer, cols, running,
        flops=10**9,
    )
    half, gain_sum = call(join_kernel, [((2, HEAD_DIM, HEAD_DIM), F32), ((LOCAL, HEAD_DIM), F32)], *back_y)
    half_other = send(half, SWAP)
    grad_keys, grad_values, grad_gain = call(
        final_kernel,
        [(tokens, BF16)] * 2 + [((LOCAL, HEAD_DIM), F32)],
        keys, values, cols, half, half_other, zeroth_back, first, grad_k, grad_v, gain_sum,
    )
    grad_levels = jnp.transpose(levels, (1, 0, 2))
    return (layer_out, grad_queries, grad_keys, grad_values, grad_levels, grad_gate, grad_gain)


def solution(mesh):
    rows = P("head", "seq", None)
    in_specs = (rows, rows, rows, P("head", "seq"), P("head", None, "seq"), rows, P("head", None), rows)
    out_specs = (rows, rows, rows, rows, P("head", None, "seq"), rows, P("head", None))
    return jax.shard_map(layer, mesh=mesh, in_specs=in_specs, out_specs=out_specs, check_vma=False)
```

```python
import jax
import jax.numpy as jnp
from jax import lax
from jax.experimental import pallas as pl
from jax.experimental.pallas import tpu as pltpu
from jax.sharding import PartitionSpec as P


HEADS = 32
HEAD_DIM = 128
TOTAL = HEADS * HEAD_DIM
EPSILON = 1e-05
F32 = jnp.float32
BF16 = jnp.bfloat16

LOCAL = 4
WIDTH = 256
DEPTH = 8
INTER = 5
LEVELS = 21
ROWS = HEAD_DIM + 8


def place():
    me = lax.axis_index("seq")
    return me // 8, lax.rem(me // 2, 4), lax.rem(me, 2)


def ring(function):
    pairs = []
    for x in range(4):
        for y in range(4):
            for core in range(2):
                to = function(x, y, core)
                if to is not None:
                    pairs.append(((x * 4 + y) * 2 + core, (to[0] * 4 + to[1]) * 2 + to[2]))
    return pairs


SWAP = ring(lambda x, y, core: (x, y, 1 - core))
UP = ring(lambda x, y, core: (x, y, 1) if core == 0 else None)
DOWN = ring(lambda x, y, core: (x, y, 0) if core == 1 else None)


Z_PAIRS = ((0, 1), (2, 3), (4, 5), (6, 7))
Z_FAR = ((1, 4), (3, 6), (5, 0), (7, 2))
Z_NEXT = ((1, 2), (3, 4), (5, 6), (7, 0))
Z_TWO = [(z, (z + 6 + 4 * (z % 2)) % 8) for z in range(8)]


def both_ways(pairs):
    return [pair for a, b in pairs for pair in ((a, b), (b, a))]


def along_z(array, pairs):
    return lax.ppermute(array, "head", pairs)


def along_y(step):
    return ring(lambda x, y, core: (x, (y + step) % 4, core))


def along_x(step):
    return ring(lambda x, y, core: ((x + step) % 4, y, core))


def send(array, pairs):
    return lax.ppermute(array, "seq", pairs)


def split(array):
    high = array.astype(BF16)
    return high, (array - high.astype(F32)).astype(BF16)


def flag(condition):
    return condition.astype(F32)


def dot(a, b, dims, precision=None):
    return lax.dot_general(a, b, (dims, ((), ())), precision=precision, preferred_element_type=F32)


NN = ((1,), (0,))
NT = ((1,), (1,))
TN = ((0,), (0,))


def iotas(shape):
    return lax.broadcasted_iota(jnp.int32, shape, 0), lax.broadcasted_iota(jnp.int32, shape, 1)


def state_kernel(
    decay_hbm, k_hbm, v_hbm, keep_ref, send_ref, run_ref, decay_ref, k_ref, v_ref, rows_ref, sems
):
    copies = [pltpu.make_async_copy(decay_hbm, decay_ref, sems.at[0])]
    for head in range(LOCAL):
        copies.append(pltpu.make_async_copy(v_hbm.at[head], v_ref.at[head], sems.at[1 + 2 * head]))
        copies.append(pltpu.make_async_copy(k_hbm.at[head], k_ref.at[head], sems.at[2 + 2 * head]))
    for copy in copies:
        copy.start()
    core = place()[2]
    early, late = iotas((WIDTH, WIDTH))
    upper = (early <= late).astype(F32).astype(BF16)
    copies[0].wait()
    decay = decay_ref[...]
    first = decay.astype(BF16).astype(F32)
    second = (decay - first).astype(BF16).astype(F32)
    rows_ref[0:4, :] = first
    rows_ref[4:8, :] = second
    rows_ref[8:12, :] = decay - first - second
    rows_ref[12:16, :] = jnp.zeros((4, WIDTH), F32)
    parts = dot(rows_ref[...].astype(BF16), upper, NN)
    running = parts[0:4, :] + parts[4:8, :] + parts[8:12, :]
    run_ref[...] = running
    rows_ref[0:4, :] = jnp.exp(running[:, WIDTH - 1 :] - running)
    tails = jnp.transpose(rows_ref[...])
    for head in range(LOCAL):
        for copy in copies[1 + 2 * head : 3 + 2 * head]:
            copy.wait()
        weighted = v_ref[head].astype(F32) * tails[:, head : head + 1]
        both = dot(k_ref[head], jnp.concatenate(split(weighted), axis=1), TN)
        state = both[:, 0:HEAD_DIM] + both[:, HEAD_DIM:]
        total = jnp.broadcast_to(running[head : head + 1, WIDTH - 1 :], (4, HEAD_DIM))
        totals = jnp.broadcast_to(running[:, WIDTH - 1 :], (4, HEAD_DIM))

        def put(ref):
            ref[head % 2, 0:HEAD_DIM, :] = state
            ref[head % 2, HEAD_DIM : HEAD_DIM + 4, :] = total
            ref[head % 2, HEAD_DIM + 4 :, :] = totals

        pl.when(core == head // 2)(lambda: put(keep_ref))
        pl.when(core != head // 2)(lambda: put(send_ref))


def pair_kernel(keep_ref, first_ref, chip_ref):
    late = place()[2] == 1
    before = jnp.where(late, first_ref[...], keep_ref[...])
    after = jnp.where(late, keep_ref[...], first_ref[...])
    carry = jnp.exp(after[:, HEAD_DIM : HEAD_DIM + 1, :])
    chip_ref[:, 0:HEAD_DIM, :] = carry * before[:, 0:HEAD_DIM, :] + after[:, 0:HEAD_DIM, :]
    chip_ref[:, HEAD_DIM:, :] = before[:, HEAD_DIM:, :] + after[:, HEAD_DIM:, :]


def intra_kernel(
    q_ref, k_ref, v_ref, level_ref, run_ref, inner_ref, mix_ref, weight_ref, scored_ref, cols_ref, rows_ref
):
    running = run_ref[...]
    grown = jnp.exp(running)
    rows_ref[...] = jnp.zeros_like(rows_ref)
    for level in range(INTER):
        rows_ref[4 * level : 4 * level + 4, :] = level_ref[DEPTH + 1 + level] * grown
    rows_ref[20:24, :] = running
    rows_ref[24:28, :] = jnp.exp(running[:, WIDTH - 1 :] - running)
    cols_ref[...] = jnp.transpose(rows_ref[...])
    early, late = iotas((WIDTH, WIDTH))
    crossed = jnp.bitwise_xor(early, late)
    causal = early <= late
    for head in range(LOCAL):
        spread = run_ref[head : head + 1, :] - cols_ref[:, 20 + head : 21 + head]
        decay = jnp.where(causal, jnp.exp(jnp.where(causal, spread, 0.0)), 0.0)
        chosen = jnp.broadcast_to(level_ref[0, head : head + 1, :], (WIDTH, WIDTH))
        for level in range(1, DEPTH + 1):
            chosen = jnp.where(crossed >= 2 ** (level - 1), level_ref[level, head : head + 1, :], chosen)
        scored = dot(k_ref[head], q_ref[head], NT)
        weight = decay * chosen
        mixing = (scored * weight).astype(BF16)
        weight_ref[head] = weight
        scored_ref[head] = scored * decay
        mix_ref[head] = mixing
        inner_ref[head] = dot(mixing, v_ref[head], TN)


def order(position, step):
    return lax.rem(position + 4 - step, 4)


def y_kernel(own_ref, one_ref, two_ref, three_ref, next_ref, bucket_ref, info_ref):
    y = place()[1]
    refs = (own_ref, one_ref, two_ref, three_ref)
    where = [order(y, step) for step in range(4)]
    totals = [ref[:, HEAD_DIM : HEAD_DIM + 1, :] for ref in refs]
    by_y = [sum(flag(where[i] == j) * totals[i] for i in range(4)) for j in range(4)]
    carry = jnp.exp(by_y[1])
    whole = jnp.zeros((2, HEAD_DIM, HEAD_DIM), F32)
    pair = jnp.zeros((2, HEAD_DIM, HEAD_DIM), F32)
    for i in range(4):
        state = refs[i][:, 0:HEAD_DIM, :]
        later = sum(flag(j > where[i]) * by_y[j] for j in range(1, 4))
        whole = whole + jnp.exp(later) * state
        if i:
            part = flag(y >= 2) * (flag(where[i] == 1) + flag(where[i] == 0) * carry)
            pair = pair + part * state
    below = sum(flag(j < y) * by_y[j] for j in range(3))
    next_ref[:, 0:HEAD_DIM, :] = whole
    next_ref[:, HEAD_DIM:, :] = jnp.broadcast_to(by_y[0] + by_y[1] + by_y[2] + by_y[3], (2, 8, HEAD_DIM))
    bucket_ref[0, :, 0:HEAD_DIM, :] = flag(lax.rem(y, 2) == 1) * one_ref[:, 0:HEAD_DIM, :]
    bucket_ref[0, :, HEAD_DIM:, :] = jnp.zeros((2, 8, HEAD_DIM), F32)
    bucket_ref[1, :, 0:HEAD_DIM, :] = pair
    bucket_ref[1, :, HEAD_DIM:, :] = jnp.broadcast_to(flag(y == 3) * by_y[2], (2, 8, HEAD_DIM))
    for j in range(4):
        info_ref[:, j : j + 1, :] = by_y[j]
    info_ref[:, 4:8, :] = jnp.broadcast_to(below, (2, 4, HEAD_DIM))


def x_kernel(own_ref, one_ref, two_ref, three_ref, info_ref, bucket_ref, wide_ref):
    x = place()[0]
    refs = (own_ref, one_ref, two_ref, three_ref)
    where = [order(x, step) for step in range(4)]
    totals = [ref[:, HEAD_DIM : HEAD_DIM + 1, :] for ref in refs]
    by_x = [sum(flag(where[i] == j) * totals[i] for i in range(4)) for j in range(4)]
    carry = jnp.exp(by_x[1])
    pair = jnp.zeros((2, HEAD_DIM, HEAD_DIM), F32)
    for i in range(1, 4):
        part = flag(x >= 2) * (flag(where[i] == 1) + flag(where[i] == 0) * carry)
        pair = pair + part * refs[i][:, 0:HEAD_DIM, :]
    below = info_ref[:, 4:5, :]
    bucket_ref[0, :, 0:HEAD_DIM, :] = flag(lax.rem(x, 2) == 1) * one_ref[:, 0:HEAD_DIM, :]
    bucket_ref[0, :, HEAD_DIM:, :] = jnp.broadcast_to(below, (2, 8, HEAD_DIM))
    bucket_ref[1, :, 0:HEAD_DIM, :] = pair
    bucket_ref[1, :, HEAD_DIM:, :] = jnp.broadcast_to(below + flag(x == 3) * by_x[2], (2, 8, HEAD_DIM))
    for j in range(4):
        wide_ref[:, j : j + 1, :] = by_x[j]
        wide_ref[:, 4 + j : 5 + j, :] = by_x[j]


def through(q, parts, cols_ref, head, levels):
    bucket, finer = (jnp.concatenate([part[i] for part in parts], axis=1) for i in range(2))
    found = dot(q, bucket, NN) + dot(q, finer, NN)
    outer = sum(
        cols_ref[:, 4 * level + head : 4 * level + head + 1] * found[:, HEAD_DIM * i : HEAD_DIM * (i + 1)]
        for i, level in enumerate(levels)
    )
    return bucket, finer, outer


def chosen_bucket(own_ref, other_ref, at, head, core):
    return jnp.where(core == head // 2, own_ref[at, head % 2], other_ref[at, head % 2])


def near_kernel(
    q_ref, inner_ref, gate_ref, grad_ref, gain_ref, cols_ref, own_ref, other_ref, first_ref, rest_ref,
    mixed_ref, act_ref, pulled_ref, bucket_ref, finer_ref, shift_ref, scaled_ref, turned_ref,
):
    core = place()[2]
    odd = flag(core == 1)
    for head in range(LOCAL):
        slot = head % 2
        zeroth = rest_ref[slot, 0:HEAD_DIM, :] if head < 2 else first_ref[slot, 0:HEAD_DIM, :]
        earlier = odd * first_ref[0, HEAD_DIM + 4 + head : HEAD_DIM + 5 + head, :]
        parts = [split(odd * zeroth)]
        shift_ref[head] = jnp.ones((8, HEAD_DIM), F32)
        shift_ref[head, 7:8, :] = earlier
        for level in (1, 2):
            chosen = chosen_bucket(own_ref, other_ref, level - 1, head, core)
            shift = jnp.exp(earlier + chosen[HEAD_DIM : HEAD_DIM + 1, :])
            shift_ref[head, level : level + 1, :] = shift
            parts.append(split(chosen[0:HEAD_DIM, :] * shift))
        bucket_ref[head], finer_ref[head], outer = through(q_ref[head], parts, cols_ref, head, (0, 1, 2))
        mixed_ref[head] = inner_ref[head] + outer
        gate = gate_ref[head].astype(F32)
        act = gate * jax.nn.sigmoid(gate)
        act_ref[head] = act
        pulled_ref[head] = grad_ref[head].astype(F32) * gain_ref[head : head + 1, :] * act
        wide_q = q_ref[head].astype(F32)
        for level in (3, 4):
            scaled = cols_ref[:, 4 * level + head : 4 * level + head + 1] * wide_q
            high, low = split(scaled)
            at = 3 * HEAD_DIM * (level - 3)
            for i, part in enumerate((high, low, high)):
                scaled_ref[head, :, at + HEAD_DIM * i : at + HEAD_DIM * (i + 1)] = part
            high, low = split(jnp.transpose(scaled))
            turned_ref[head, level - 3, :, 0:WIDTH] = high
            turned_ref[head, level - 3, :, WIDTH:] = low


def mixed_kernel(
    scaled_ref, near_ref, act_ref, pulled_ref, own_ref, other_ref, shifts_ref,
    mixed_ref, pay_ref, bucket_ref, finer_ref, shift_ref,
):
    core = place()[2]
    ones = jnp.ones((8, HEAD_DIM), BF16)
    squares = jnp.zeros((8, WIDTH), F32)
    crosses = jnp.zeros((8, WIDTH), F32)
    for head in range(LOCAL):
        earlier = shifts_ref[head, 7:8, :]
        shift_ref[head] = shifts_ref[head]
        parts = []
        for level in (3, 4):
            chosen = chosen_bucket(own_ref, other_ref, level - 3, head, core)
            shift = jnp.exp(earlier + chosen[HEAD_DIM : HEAD_DIM + 1, :])
            shift_ref[head, level : level + 1, :] = shift
            parts.append(split(chosen[0:HEAD_DIM, :] * shift))
        for i, (high, low) in enumerate(parts):
            piece = slice(HEAD_DIM * i, HEAD_DIM * (i + 1))
            bucket_ref[head, :, piece] = high
            finer_ref[head, :, piece] = low
        stacked = jnp.concatenate([part for high, low in parts for part in (high, high, low)], axis=0)
        mixed = near_ref[head] + dot(scaled_ref[head], stacked, NN)
        mixed_ref[head] = mixed
        gated = mixed * act_ref[head]
        squares = squares + dot(ones, (gated * gated).astype(BF16), NT)
        crosses = crosses + dot(ones, (mixed * pulled_ref[head]).astype(BF16), NT)
    for half in range(2):
        piece = slice(HEAD_DIM * half, HEAD_DIM * (half + 1))
        pay_ref[half : half + 1, :] = squares[0:1, piece]
        pay_ref[2 + half : 3 + half, :] = crosses[0:1, piece]


def add_kernel(a_ref, b_ref, out_ref):
    out_ref[...] = a_ref[...] + b_ref[...]


def gate_kernel(
    turned_ref, mixed_ref, act_ref, pulled_ref, grad_ref, shift_ref, sums_ref, three_ref, two_ref, one_ref,
    g_ref, scale_ref, keep_ref, send_ref,
):
    x, _, core = place()
    sums = (sums_ref[...] + three_ref[...]) + (two_ref[...] + one_ref[...])
    first = sums.astype(BF16).astype(F32)
    second = (sums - first).astype(BF16).astype(F32)
    parts = jnp.concatenate([first, second, sums - first - second, jnp.zeros_like(sums)], axis=0).astype(BF16)
    row, column = iotas((16, 4 * HEAD_DIM))
    chosen = ((row < 12) & (lax.rem(row, 4) == column // HEAD_DIM)).astype(F32).astype(BF16)
    wide = dot(parts, chosen, TN)
    squares = jnp.concatenate([wide[:, 0:HEAD_DIM], wide[:, HEAD_DIM : 2 * HEAD_DIM]], axis=0)
    crosses = jnp.concatenate([wide[:, 2 * HEAD_DIM : 3 * HEAD_DIM], wide[:, 3 * HEAD_DIM :]], axis=0)
    inverse = lax.rsqrt(squares * (1.0 / TOTAL) + EPSILON)
    pull = inverse * inverse * inverse * crosses * (1.0 / TOTAL)
    scale_ref[0] = inverse
    scale_ref[1] = pull
    gains = []
    for ref in (keep_ref, send_ref):
        ref[:, :, HEAD_DIM:, :] = jnp.zeros((2, 2, 8, HEAD_DIM), F32)
    for head in range(LOCAL):
        act = act_ref[head]
        gated = mixed_ref[head] * act
        gains.append(jnp.sum(grad_ref[head].astype(F32) * (gated * inverse), axis=0, keepdims=True))
        g = (inverse * pulled_ref[head] - gated * act * pull).astype(BF16)
        g_ref[head] = g
        twice = jnp.concatenate([g, g], axis=0)
        far = [dot(turned_ref[head, i], twice, NN) * shift_ref[head, 3 + i : 4 + i, :] for i in range(2)]
        near = jnp.where(lax.rem(x, 2) == 1, far[0], far[1])

        def put(ref):
            ref[0, head % 2, 0:HEAD_DIM, :] = near
            ref[1, head % 2, 0:HEAD_DIM, :] = far[1]

        pl.when(core == head // 2)(lambda: put(keep_ref))
        pl.when(core != head // 2)(lambda: put(send_ref))
    for head in range(LOCAL):
        for ref in (keep_ref, send_ref):
            ref[0, 0, HEAD_DIM + head : HEAD_DIM + head + 1, :] = gains[head]
            ref[1, 0, HEAD_DIM + head : HEAD_DIM + head + 1, :] = gains[head]


def reached(q, g, cols_ref, shift_ref, head, levels):
    parts = [split(cols_ref[:, 4 * level + head : 4 * level + head + 1] * g) for level in levels]
    both = dot(q, jnp.concatenate([part for pair in parts for part in pair], axis=1), TN)
    found = []
    for i, level in enumerate(levels):
        at = 2 * HEAD_DIM * i
        grad = both[:, at : at + HEAD_DIM] + both[:, at + HEAD_DIM : at + 2 * HEAD_DIM]
        found.append(grad * shift_ref[head, level : level + 1, :])
    return found


def meet_kernel(keep_ref, other_ref, near_ref, far_ref):
    near_ref[...] = keep_ref[0] + other_ref[0]
    far_ref[...] = keep_ref[1] + other_ref[1]


def close_kernel(
    q_ref, g_ref, mixed_ref, gate_ref, grad_ref, gain_ref, cols_ref, shift_ref, scale_ref,
    out_ref, grad_gate_ref, keep_ref, send_ref, zeroth_ref,
):
    core = place()[2]
    inverse, pull = scale_ref[0], scale_ref[1]
    for ref in (keep_ref, send_ref):
        ref[:, :, HEAD_DIM:, :] = jnp.zeros((2, 2, 8, HEAD_DIM), F32)
    for head in range(LOCAL):
        near = reached(q_ref[head], g_ref[head].astype(F32), cols_ref, shift_ref, head, (0, 1, 2))
        zeroth_ref[head] = near[0]

        def put(ref):
            ref[0, head % 2, 0:HEAD_DIM, :] = near[1]
            ref[1, head % 2, 0:HEAD_DIM, :] = near[2]

        pl.when(core == head // 2)(lambda: put(keep_ref))
        pl.when(core != head // 2)(lambda: put(send_ref))
    for head in range(LOCAL):
        gain = gain_ref[head : head + 1, :]
        gate = gate_ref[head].astype(F32)
        sigmoid = jax.nn.sigmoid(gate)
        mixed = mixed_ref[head]
        gated = mixed * (gate * sigmoid)
        out_ref[head] = (gain * (gated * inverse)).astype(BF16)
        grad_gated = inverse * (grad_ref[head].astype(F32) * gain) - gated * pull
        grad_gate_ref[head] = (grad_gated * mixed * sigmoid * (1.0 + gate * (1.0 - sigmoid))).astype(BF16)


def down_kernel(
    own_ref, one_ref, two_ref, three_ref, near_ref, near_other_ref, info_ref, wide_ref,
    m0_ref, m1_ref, m2_ref, m3_ref,
):
    x, y, _ = place()
    refs = (own_ref, one_ref, two_ref, three_ref)
    carry_x = jnp.exp(wide_ref[:, 1:2, :])
    first = x == 0
    c1 = flag(x <= 2)
    c2 = flag(first) * carry_x + flag(x == 1)
    c3 = flag(first) * carry_x
    body = slice(0, HEAD_DIM)
    state = c1 * one_ref[:, body, :] + c2 * two_ref[:, body, :] + c3 * three_ref[:, body, :]
    tails = [ref[:, HEAD_DIM:, :] for ref in refs]
    where = [lax.rem(x + step, 4) for step in range(4)]
    by_x = [sum(flag(where[i] == j) * tails[i] for i in range(4)) for j in range(4)]
    gains = ((by_x[0] + by_x[1]) + by_x[2]) + by_x[3]
    low = near_ref[0, :, body, :] + near_other_ref[0, :, body, :]
    high = near_ref[1, :, body, :] + near_other_ref[1, :, body, :]
    totals = [info_ref[:, j : j + 1, :] for j in range(4)]
    after = [totals[1] + totals[2] + totals[3], totals[2] + totals[3], totals[3], jnp.zeros_like(totals[3])]
    after = [jnp.exp(part) for part in after]
    carry_y = jnp.exp(totals[1])
    for step, ref in enumerate((m0_ref, m1_ref, m2_ref, m3_ref)):
        to = order(y, step)
        message = sum(flag(to == j) * after[j] for j in range(4)) * state
        if step == 1:
            message = message + flag(lax.rem(y, 2) == 1) * low
        if step:
            message = message + flag(y >= 2) * (flag(to == 1) + flag(to == 0) * carry_y) * high
        ref[:, body, :] = message
        ref[:, HEAD_DIM:, :] = gains


def backward_kernel(
    q_ref, k_ref, v_ref, g_ref, mix_ref, weight_ref, scored_ref, bucket_ref, finer_ref, far_ref, far_finer_ref, cols_ref, run_ref,
    grad_q_ref, grad_k_ref, grad_v_ref, levels_ref,
):
    early, late = iotas((WIDTH, WIDTH))
    crossed = jnp.bitwise_xor(early, late)
    ones = jnp.ones((8, HEAD_DIM), BF16)
    for level in range(DEPTH + 1 + INTER, LEVELS):
        levels_ref[level] = jnp.zeros((LOCAL, WIDTH), F32)
    for head in range(LOCAL):
        q, k, v, g = q_ref[head], k_ref[head], v_ref[head], g_ref[head]
        grad_mixing = dot(v, g, NT)
        grad_scores = (grad_mixing * weight_ref[head]).astype(BF16)
        grad_k_ref[head] = dot(grad_scores, q, NN)
        grad_v_ref[head] = dot(mix_ref[head], g, NN)
        grad_q = dot(grad_scores, k, TN)
        moved = grad_mixing * scored_ref[head]
        for level in range(DEPTH + 1):
            inside = crossed == 0
            if level:
                inside = (crossed >= 2 ** (level - 1)) & (crossed < 2**level)
            levels_ref[level, head : head + 1, :] = jnp.sum(jnp.where(inside, moved, 0.0), axis=0, keepdims=True)
        wide_q = q.astype(F32)
        grown = jnp.exp(run_ref[head : head + 1, :])
        for level in range(INTER):
            high, low = (bucket_ref, finer_ref) if level < 3 else (far_ref, far_finer_ref)
            piece = slice(HEAD_DIM * (level % 3), HEAD_DIM * (level % 3 + 1))
            pulled = dot(g, high[head, :, piece], NT) + dot(g, low[head, :, piece], NT)
            at = 4 * level + head
            grad_q = grad_q + cols_ref[:, at : at + 1] * pulled
            high, low = split(wide_q * pulled)
            sums = dot(ones, high, NT) + dot(ones, low, NT)
            levels_ref[DEPTH + 1 + level, head : head + 1, :] = grown * sums[0:1, :]
        grad_q_ref[head] = grad_q.astype(BF16)


def join_kernel(own_ref, one_ref, two_ref, three_ref, half_ref, sum_ref):
    y = place()[1]
    refs = (own_ref, one_ref, two_ref, three_ref)
    where = [lax.rem(y + step, 4) for step in range(4)]
    tails = [ref[0, HEAD_DIM : HEAD_DIM + LOCAL, :] for ref in refs]
    by_y = [sum(flag(where[i] == j) * tails[i] for i in range(4)) for j in range(4)]
    sum_ref[...] = ((by_y[0] + by_y[1]) + by_y[2]) + by_y[3]
    half_ref[...] = sum(ref[:, 0:HEAD_DIM, :] for ref in refs)


def final_kernel(
    k_ref, v_ref, cols_ref, half_ref, other_ref, zeroth_ref, first_ref, grad_k_ref, grad_v_ref, sum_ref,
    out_k_ref, out_v_ref, gain_ref,
):
    gain_ref[...] = sum_ref[...]
    core = place()[2]
    even = core == 0
    for head in range(LOCAL):
        slot = head % 2
        half = jnp.where(core == head // 2, half_ref[slot], other_ref[slot])
        carry = jnp.exp(first_ref[0, HEAD_DIM + 4 + head : HEAD_DIM + 5 + head, :])
        state = jnp.where(even, carry * half + zeroth_ref[head], half).astype(BF16)
        tail = cols_ref[:, 24 + head : 25 + head]
        k, v = k_ref[head], v_ref[head]
        out_k_ref[head] = (grad_k_ref[head] + tail * dot(v, state, NT)).astype(BF16)
        out_v_ref[head] = (grad_v_ref[head] + tail * dot(k, state, NN)).astype(BF16)


def call(kernel, outs, *args, scratch=(), flops=0, hbm=(), limit=12):
    size = sum(a.size * a.dtype.itemsize for a in args)
    shapes = [jax.ShapeDtypeStruct(shape, kind) for shape, kind in outs]
    size += sum(s.size * s.dtype.itemsize for s in shapes)
    spaces = [pltpu.HBM if i in hbm else pltpu.VMEM for i in range(len(args))]
    return pl.pallas_call(
        kernel,
        out_shape=shapes,
        in_specs=[pl.BlockSpec(memory_space=space) for space in spaces],
        scratch_shapes=list(scratch),
        cost_estimate=pl.CostEstimate(flops=flops, bytes_accessed=size, transcendentals=0),
        compiler_params=pltpu.CompilerParams(vmem_limit_bytes=limit * 2**20),
    )(*args)


def layer(queries, keys, values, log_decay, level_weight, gate_input, norm_gain, out_grad):
    level_rows = jnp.transpose(level_weight, (1, 0, 2))
    message = ((2, ROWS, HEAD_DIM), F32)
    double = ((2, 2, ROWS, HEAD_DIM), F32)
    tokens = (LOCAL, WIDTH, HEAD_DIM)
    square = (LOCAL, WIDTH, WIDTH)
    info = ((2, 8, HEAD_DIM), F32)
    columns = ((WIDTH, HEAD_DIM), F32)

    keep, away, running = call(
        state_kernel,
        [message, message, ((LOCAL, WIDTH), F32)],
        *(pltpu.with_memory_space_constraint(a, pltpu.HBM) for a in (log_decay, keys, values)),
        scratch=[
            pltpu.VMEM((LOCAL, WIDTH), F32), pltpu.VMEM(tokens, BF16), pltpu.VMEM(tokens, BF16),
            pltpu.VMEM((16, WIDTH), F32), pltpu.SemaphoreType.DMA((1 + 2 * LOCAL,)),
        ],
        hbm=(0, 1, 2),
    )
    first = send(away, SWAP)
    (chip,) = call(pair_kernel, [message], keep, first)
    from_y = [send(chip, along_y(step)) for step in (1, 2, 3)]
    rest = send(keep, UP)
    inner, mixing, weight, scored, cols = call(
        intra_kernel,
        [(tokens, F32), (square, BF16), (square, F32), (square, F32), columns],
        queries, keys, values, level_rows, running,
        scratch=[pltpu.VMEM((HEAD_DIM, WIDTH), F32)],
        flops=10**9,
    )
    row, near, totals_y = call(y_kernel, [message, double, info], chip, *from_y)
    from_x = [send(row, along_x(step)) for step in (1, 2, 3)]
    near_other = send(near, SWAP)
    far, totals_x = call(x_kernel, [double, info], row, *from_x, totals_y)
    far_other = send(far, SWAP)
    near_kind = ((LOCAL, HEAD_DIM, 3 * HEAD_DIM), BF16)
    far_kind = ((LOCAL, HEAD_DIM, 2 * HEAD_DIM), BF16)
    rows = ((LOCAL, 8, HEAD_DIM), F32)
    scaled_kind = ((LOCAL, WIDTH, 6 * HEAD_DIM), BF16)
    turned_kind = ((LOCAL, 2, HEAD_DIM, 2 * WIDTH), BF16)
    near_mixed, act, pulled, bucket, finer, shifts, scaled_q, turned_q = call(
        near_kernel,
        [(tokens, F32)] * 3 + [near_kind, near_kind, rows, scaled_kind, turned_kind],
        queries, inner, gate_input, out_grad, norm_gain, cols, near, near_other, first, rest,
        flops=10**9,
    )
    mixed, pay, far_bucket, far_finer, shift = call(
        mixed_kernel,
        [(tokens, F32), ((4, HEAD_DIM), F32), far_kind, far_kind, rows],
        scaled_q, near_mixed, act, pulled, far, far_other, shifts,
    )
    (pay,) = call(add_kernel, [((4, HEAD_DIM), F32)], pay, along_z(pay, both_ways(Z_PAIRS)))
    others = [along_z(pay, pairs) for pairs in (both_ways(Z_FAR), Z_TWO, both_ways(Z_NEXT))]
    grad_mixed, scale, far_keep, far_away = call(
        gate_kernel,
        [(tokens, BF16), ((2, WIDTH, HEAD_DIM), F32), double, double],
        turned_q, mixed, act, pulled, out_grad, shift, pay, *others,
    )
    to_one, to_far = call(meet_kernel, [message] * 2, far_keep, send(far_away, SWAP))
    back_x = [send(to_one, along_x(-1)), send(to_far, along_x(-2)), send(to_far, along_x(-3))]
    layer_out, grad_gate, near_keep, near_away, zeroth = call(
        close_kernel,
        [(tokens, BF16)] * 2 + [double] * 2 + [((LOCAL, HEAD_DIM, HEAD_DIM), F32)],
        queries, grad_mixed, mixed, gate_input, out_grad, norm_gain, cols, shift, scale,
        flops=10**9,
    )
    near_back = send(near_away, SWAP)
    messages = call(down_kernel, [message] * 4, to_far, *back_x, near_keep, near_back, totals_y, totals_x)
    back_y = [messages[0]] + [send(messages[step], along_y(-step)) for step in (1, 2, 3)]
    zeroth_back = send(zeroth, DOWN)
    grad_queries, grad_k, grad_v, levels = call(
        backward_kernel,
        [(tokens, BF16), (tokens, F32), (tokens, F32), ((LEVELS, LOCAL, WIDTH), F32)],
        queries, keys, values, grad_mixed, mixing, weight, scored, bucket, finer, far_bucket, far_finer, cols, running,
        flops=10**9,
    )
    half, gain_sum = call(join_kernel, [((2, HEAD_DIM, HEAD_DIM), F32), ((LOCAL, HEAD_DIM), F32)], *back_y)
    half_other = send(half, SWAP)
    grad_keys, grad_values, grad_gain = call(
        final_kernel,
        [(tokens, BF16)] * 2 + [((LOCAL, HEAD_DIM), F32)],
        keys, values, cols, half, half_other, zeroth_back, first, grad_k, grad_v, gain_sum,
    )
    grad_levels = jnp.transpose(levels, (1, 0, 2))
    return (layer_out, grad_queries, grad_keys, grad_values, grad_levels, grad_gate, grad_gain)


def solution(mesh):
    rows = P("head", "seq", None)
    in_specs = (rows, rows, rows, P("head", "seq"), P("head", None, "seq"), rows, P("head", None), rows)
    out_specs = (rows, rows, rows, rows, P("head", None, "seq"), rows, P("head", None))
    return jax.shard_map(layer, mesh=mesh, in_specs=in_specs, out_specs=out_specs, check_vma=False)
```
